32 devices in a mesh: seq: 8 (over z, y), fsdp: 4 (over x, core).
Axes of the slice: x: 2, y: 2, z: 4, core: 2. Of those that a mesh axis runs over, the one named last changes fastest.
Arguments:
- hidden_in: bfloat16 [4, 2048, 1024], P('fsdp', 'seq'), may hold values from -6 to 6
- block_counts: int32 [4, 8], P('fsdp', 'seq'), may hold values from 1 to 256, as said below
- seq_starts: int32 [4, 8], P('fsdp', 'seq'), may hold values from 0 to 1, as said below
- decay_rates: float32 [8], replicated, as said below
- w_query: bfloat16 [1024, 1024], P(('seq', 'fsdp')), may hold values from -0.1875 to 0.1875
- w_key: bfloat16 [1024, 1024], P(('seq', 'fsdp')), may hold values from -0.1875 to 0.1875
- w_value: bfloat16 [1024, 1024], P(('seq', 'fsdp')), may hold values from -0.1875 to 0.1875
- w_gate: bfloat16 [1024, 1024], P(('seq', 'fsdp')), may hold values from -0.1875 to 0.1875
- w_out: bfloat16 [1024, 1024], P(('seq', 'fsdp')), may hold values from -0.375 to 0.375
- w_left: bfloat16 [1024, 2816], P(('seq', 'fsdp')), may hold values from -0.1875 to 0.1875
- w_right: bfloat16 [1024, 2816], P(('seq', 'fsdp')), may hold values from -0.1875 to 0.1875
- w_down: bfloat16 [2816, 1024], P(('seq', 'fsdp')), may hold values from -0.109375 to 0.109375
- cotangent: bfloat16 [4, 2048, 1024], P('fsdp', 'seq'), may hold values from -6 to 6
Outputs:
- output: bfloat16 [4, 2048, 1024], P('fsdp', 'seq')
- grad_input: float32 [4, 2048, 1024], P('fsdp', 'seq')
- grad_w_query: float32 [1024, 1024], P(('seq', 'fsdp'))
- grad_w_key: float32 [1024, 1024], P(('seq', 'fsdp'))
- grad_w_value: float32 [1024, 1024], P(('seq', 'fsdp'))
- grad_w_gate: float32 [1024, 1024], P(('seq', 'fsdp'))
- grad_w_out: float32 [1024, 1024], P(('seq', 'fsdp'))
- grad_w_left: float32 [1024, 2816], P(('seq', 'fsdp'))
- grad_w_right: float32 [1024, 2816], P(('seq', 'fsdp'))
- grad_w_down: float32 [2816, 1024], P(('seq', 'fsdp'))
The draws below stay inside these ranges and needn't reach their ends.
Inputs may be any that keep to these rules, and one draw needn't show every extreme that they name: `seq_starts`: 1 marks the first block of a sequence: every group's first block, and otherwise only blocks whose index in the group is a multiple of 4. `block_counts`: every block is full except the last block of a sequence. `decay_rates`: fixed constants of the layer; no gradient is taken for them.
All inputs are finite; a program needn't handle non-finite values.
Results may differ from the reference program's by a relative error of at most 0.013.
Values may be sent and summed in bfloat16 or wider, within the bound.
A program may use at most 104 MiB of HBM per device.

```python
import jax
import jax.numpy as jnp
from jax import lax

D = 1024
HEADS = 8
HEAD = 128
FF = 2816
BLOCK = 256
MIN_BLOCKS = 4
GROUP_BLOCKS = 8
CHAIN = 2048
GROUPS = 4


def sequence_plan(key):
    coin_key = jax.random.fold_in(key, 101)
    fill_key = jax.random.fold_in(key, 202)
    index = jnp.arange(GROUP_BLOCKS)
    coins = jax.random.randint(coin_key, (GROUPS, GROUP_BLOCKS), 0, 2)
    aligned = (index % MIN_BLOCKS == 0)[None, :]
    first = (index == 0)[None, :]
    starts = jnp.where(first, 1, jnp.where(aligned, coins, 0)).astype(jnp.int32)
    following = jnp.concatenate([starts[:, 1:], jnp.ones((GROUPS, 1), jnp.int32)], axis=1)
    partial_fill = jax.random.randint(fill_key, (GROUPS, GROUP_BLOCKS), 1, BLOCK + 1)
    counts = jnp.where(following == 1, partial_fill, BLOCK).astype(jnp.int32)
    return (counts, starts)


def draw_block_counts(key, part):
    return sequence_plan(key)[0]


def draw_seq_starts(key, part):
    return sequence_plan(key)[1]


def draw_decay_rates(key, part):
    pick_key = jax.random.fold_in(key, 303)
    fast_key = jax.random.fold_in(key, 404)
    slow_key = jax.random.fold_in(key, 505)
    slow_heads = jax.random.randint(pick_key, (HEADS,), 0, 2) == 1
    fast_rate = jax.random.uniform(fast_key, (HEADS,), jnp.float32, 0.02, 0.035)
    slow_rate = jax.random.uniform(slow_key, (HEADS,), jnp.float32, 0.2, 1.5) / CHAIN
    return jnp.where(slow_heads, slow_rate, fast_rate)


def levels(rng, shape, cuts, low, high):
    gain, own = 1.0, jax.random.fold_in(rng, 6)
    for dim, blocks in cuts:
        steps = jnp.exp(jax.random.uniform(jax.random.fold_in(own, dim), (blocks,), jnp.float32, low / len(cuts), high / len(cuts)))
        gain = gain * jnp.repeat(steps, shape[dim] // blocks).reshape([-1 if axis == dim else 1 for axis in range(len(shape))])
    return gain


def centred(stream_key, dims, width, reach, shards=(), held_as=jnp.bfloat16):
    level = levels(stream_key, dims, shards, -0.22, 0.18) if shards else 1.0
    values = jax.random.normal(stream_key, dims, jnp.float32) * width * level
    return jnp.minimum(jnp.maximum(values, -reach), reach).astype(held_as)


def setup_inputs(seed: int = 0) -> dict:
    keys = jax.random.split(jax.random.key(seed), 14)
    return {
        "hidden_in": centred(keys[0], (GROUPS, CHAIN, D), 1.0, 6.0, ((0, 4), (1, 8))),
        "block_counts": draw_block_counts(jax.random.fold_in(keys[13], 71), 0),
        "seq_starts": draw_seq_starts(jax.random.fold_in(keys[13], 71), 0),
        "decay_rates": draw_decay_rates(jax.random.fold_in(keys[13], 71), 0),
        "w_query": centred(keys[4], (D, D), D ** -0.5, 0.1875, ((0, 32),)),
        "w_key": centred(keys[5], (D, D), D ** -0.5, 0.1875, ((0, 32),)),
        "w_value": centred(keys[6], (D, D), D ** -0.5, 0.1875, ((0, 32),)),
        "w_gate": centred(keys[7], (D, D), D ** -0.5, 0.1875, ((0, 32),)),
        "w_out": centred(keys[8], (D, D), (D // 4) ** -0.5, 0.375, ((0, 32),)),
        "w_left": centred(keys[9], (D, FF), D ** -0.5, 0.1875, ((0, 32),)),
        "w_right": centred(keys[10], (D, FF), D ** -0.5, 0.1875, ((0, 32),)),
        "w_down": centred(keys[11], (FF, D), FF ** -0.5, 0.109375, ((0, 32),)),
        "cotangent": centred(keys[12], (GROUPS, CHAIN, D), 1.0, 6.0, ((0, 4), (1, 8))),
    }


EPSILON = 1e-06
HIGHEST = lax.Precision.HIGHEST

@jax.custom_vjp
def low(v):
    return lax.optimization_barrier(v.astype(jnp.bfloat16)).astype(jnp.float32)

@jax.custom_vjp
def low_back(v):
    return v

def low_keep(v):
    return (low(v), None)

def low_pass(kept, grad):
    return (grad,)

def back_keep(v):
    return (v, None)

def back_low(kept, grad):
    return (low(grad),)
low.defvjp(low_keep, low_pass)
low_back.defvjp(back_keep, back_low)

def rms_norm(values):
    return values * lax.rsqrt(lax.optimization_barrier(jnp.mean(values * values, axis=-1, keepdims=True)) + EPSILON)

def attend(query, key_rows, value_rows, keep_state, decay_rates):
    position = jnp.arange(BLOCK).astype(jnp.float32)
    decay_in = jnp.exp(-(position[:, None] + 1.0) * decay_rates[None, :])
    decay_out = jnp.exp(-(BLOCK - 1.0 - position[:, None]) * decay_rates[None, :])
    decay_block = jnp.exp(-BLOCK * decay_rates)
    distance = position[:, None] - position[None, :]
    decay_mask = jnp.where(distance[None] >= 0, jnp.exp(-jnp.maximum(distance, 0.0)[None] * decay_rates[:, None, None]), 0.0)
    shape_four = (GROUP_BLOCKS, BLOCK, HEADS, HEAD)

    def block_step(state, pieces):
        query_blk, key_blk, value_blk, keep_one = pieces
        prior = state * keep_one
        raw_scores = jnp.einsum('thd,shd->hts', query_blk, key_blk, precision=HIGHEST)
        scores = low(low_back(raw_scores) * decay_mask)
        intra = jnp.einsum('hts,shd->thd', scores, value_blk, precision=HIGHEST)
        inter = jnp.einsum('thd,hde->the', query_blk * decay_in[:, :, None], prior, precision=HIGHEST)
        local = jnp.einsum('thd,the->hde', key_blk * decay_out[:, :, None], value_blk, precision=HIGHEST)
        return (decay_block[:, None, None] * prior + local, intra + inter)
    start_state = jnp.zeros((HEADS, HEAD, HEAD), jnp.float32)
    _, mixed = lax.scan(jax.checkpoint(block_step), start_state, (query.reshape(shape_four), key_rows.reshape(shape_four), value_rows.reshape(shape_four), keep_state))
    return mixed.reshape(CHAIN, D)

def layer(hidden, w_query, w_key, w_value, w_gate, w_out, w_left, w_right, w_down, token_mask, keep_state, decay_rates):
    normed_in = low(rms_norm(hidden))

    def project(weight):
        return low_back(jnp.dot(normed_in, weight, precision=HIGHEST))
    query = low(jax.nn.silu(project(w_query)))
    key_rows = low(jax.nn.silu(project(w_key)) * token_mask[:, None])
    value_rows = low(jax.nn.silu(project(w_value)))
    gate_rows = jax.nn.silu(project(w_gate))
    mixed = low_back(attend(query, key_rows, value_rows, keep_state, decay_rates))
    gated = low(rms_norm(mixed) * gate_rows)
    stream = hidden + low_back(jnp.dot(gated, w_out, precision=HIGHEST))
    normed_mid = low(rms_norm(stream))
    left_pre = low_back(jnp.dot(normed_mid, w_left, precision=HIGHEST))
    right_pre = low_back(jnp.dot(normed_mid, w_right, precision=HIGHEST))
    product = low(left_pre * right_pre)
    return token_mask[:, None] * (stream + low_back(jnp.dot(product, w_down, precision=HIGHEST)))

def reference(hidden_in, block_counts, seq_starts, decay_rates, w_query, w_key, w_value, w_gate, w_out, w_left, w_right, w_down, cotangent):
    weights = tuple((weight.astype(jnp.float32) for weight in (w_query, w_key, w_value, w_gate, w_out, w_left, w_right, w_down)))
    offsets = jnp.arange(BLOCK).astype(jnp.int32)

    def one_group(totals, pieces):
        group_in, group_counts, group_starts, group_cot = pieces
        token_mask = (offsets[None, :] < group_counts[:, None]).astype(jnp.float32).reshape(CHAIN)
        keep_state = (1 - group_starts).astype(jnp.float32)

        def run(hidden, *mats):
            return layer(hidden, *mats, token_mask, keep_state, decay_rates)
        result, pull = jax.vjp(run, group_in.astype(jnp.float32), *weights)
        grads = pull(group_cot.astype(jnp.float32))
        totals = tuple((total + grad for total, grad in zip(totals, grads[1:])))
        return (totals, (result.astype(jnp.bfloat16), grads[0]))
    zeros = tuple((jnp.zeros(weight.shape, jnp.float32) for weight in weights))
    totals, (output, grad_input) = lax.scan(one_group, zeros, (hidden_in, block_counts, seq_starts, cotangent))
    return (output, grad_input, totals[0], totals[1], totals[2], totals[3], totals[4], totals[5], totals[6], totals[7])
```

```python
import jax
import jax.numpy as jnp
from jax import lax
from jax.sharding import PartitionSpec as P

EPSILON = 1e-06
HIGHEST = lax.Precision.HIGHEST


def entering(value, axis, join, neutral):
    count, mine = (lax.axis_size(axis), lax.axis_index(axis))
    pieces = jax.tree.map(lambda part: lax.all_gather(part, axis), value)
    running = jax.tree.map(
        lambda part, zero: jnp.full_like(part, 0) + jnp.asarray(zero, part.dtype), value, neutral
    )

    def hop(position, running):
        longer = join(running, jax.tree.map(lambda part: part[position], pieces))
        return jax.tree.map(lambda new, old: jnp.where(position < mine, new, old), longer, running)

    return lax.fori_loop(0, count - 1, hop, running)


def carried_in(x, axis, join, neutral):
    count = lax.axis_size(axis)
    place = lax.axis_index(axis)
    ahead = count - 1 - place
    gathered = jax.tree.map(
        lambda a, kind: lax.all_gather(a.astype(kind), axis), x, (jnp.bfloat16, jnp.bfloat16)
    )
    state = jax.tree.map(lambda a, e: jnp.zeros_like(a) + jnp.asarray(e, a.dtype), x, neutral)

    def one(hop, state):
        source = count - 1 - hop
        return join(
            state,
            jax.tree.map(
                lambda a, own: lax.dynamic_index_in_dim(a, source, 0, False).astype(own.dtype),
                gathered,
                x,
            ),
        )

    return lax.fori_loop(0, ahead, one, state)


def rms_norm(values):
    return values * lax.rsqrt(jnp.mean(values * values, axis=-1, keepdims=True) + EPSILON)


def norm_back(values, grad_norm):
    _, pull = jax.vjp(rms_norm, values)
    return pull(grad_norm)[0]


def silu_slope(values):
    sigma = jax.nn.sigmoid(values)
    return sigma * (1.0 + values * (1.0 - sigma))


def affine_join(earlier, later):
    return (earlier[0] * later[0], later[0][:, None, None] * earlier[1] + later[1])


def matmul(left, right):
    return jnp.dot(left, right, preferred_element_type=jnp.float32)


def matmul_left_t(left, right):
    return jnp.einsum("ab,ac->bc", left, right, preferred_element_type=jnp.float32)


def matmul_right_t(left, right):
    return jnp.einsum("ab,cb->ac", left, right, preferred_element_type=jnp.float32)


def precise(form, left, right):
    return jnp.einsum(form, left, right, precision=HIGHEST)


def on_device(
    hidden_in,
    block_counts,
    seq_starts,
    decay_rates,
    w_query,
    w_key,
    w_value,
    w_gate,
    w_out,
    w_left,
    w_right,
    w_down,
    cotangent,
):
    tok_rows = hidden_in.shape[1]
    width = hidden_in.shape[2]
    heads = decay_rates.shape[0]
    head_dim = width // heads
    blocks = block_counts.shape[1]
    block_len = tok_rows // blocks
    residual_in = hidden_in[0].astype(jnp.float32)
    offsets = jnp.arange(block_len)
    token_mask = (offsets[None, :] < block_counts[0][:, None]).astype(jnp.float32).reshape(tok_rows)
    keep_state = (1 - seq_starts[0]).astype(jnp.float32)
    position = offsets.astype(jnp.float32)
    decay_in = jnp.exp(-(position[:, None] + 1.0) * decay_rates[None, :])
    decay_out = jnp.exp(-(block_len - 1.0 - position[:, None]) * decay_rates[None, :])
    decay_block = jnp.exp(-block_len * decay_rates)
    distance = position[:, None] - position[None, :]
    decay_mask = jnp.where(
        distance[None] >= 0,
        jnp.exp(-jnp.maximum(distance, 0.0)[None] * decay_rates[:, None, None]),
        0.0,
    )
    shape_four = (blocks, block_len, heads, head_dim)
    identity = (
        jnp.ones((heads,), jnp.float32),
        jnp.zeros((heads, head_dim, head_dim), jnp.float32),
    )
    rows = w_query.shape[0]
    hidden = w_left.shape[1]
    packed = jnp.concatenate(
        (w_query, w_key, w_value, w_gate, w_out, w_left, w_right, w_down.reshape(rows, hidden)),
        axis=1,
    )
    full = lax.all_gather(packed, ("seq", "fsdp"), axis=0, tiled=True)
    attn_full = tuple(full[:, n * width : (n + 1) * width] for n in range(5))
    ffn_full = (
        full[:, 5 * width : 5 * width + hidden],
        full[:, 5 * width + hidden : 5 * width + 2 * hidden],
        full[:, 5 * width + 2 * hidden :].reshape(hidden, width),
    )
    normed_in = rms_norm(residual_in).astype(jnp.bfloat16)
    query_pre = matmul(normed_in, attn_full[0])
    key_pre = matmul(normed_in, attn_full[1])
    value_pre = matmul(normed_in, attn_full[2])
    gate_pre = matmul(normed_in, attn_full[3])
    query_rows = jax.nn.silu(query_pre).astype(jnp.bfloat16)
    key_rows = (jax.nn.silu(key_pre) * token_mask[:, None]).astype(jnp.bfloat16)
    value_rows = jax.nn.silu(value_pre).astype(jnp.bfloat16)
    gate_rows = jax.nn.silu(gate_pre)
    query_blk = query_rows.reshape(shape_four)
    key_blk = key_rows.reshape(shape_four)
    value_blk = value_rows.reshape(shape_four)
    key_full = key_blk.astype(jnp.float32)
    value_full = value_blk.astype(jnp.float32)
    query_decay = query_blk.astype(jnp.float32) * decay_in[None, :, :, None]
    key_decay = key_full * decay_out[None, :, :, None]
    local_states = precise("bthd,bthe->bhde", key_decay, value_full)
    carry_scale = identity[0]
    carry_state = identity[1]
    number = 0
    factor = keep_state[number] * decay_block
    carry_scale = carry_scale * factor
    carry_state = factor[:, None, None] * carry_state + local_states[number]
    arrived = entering((carry_scale, carry_state), "seq", affine_join, identity)
    state_now = arrived[1]
    number = 0
    prior = keep_state[number] * state_now
    priors = [prior]
    prior_states = jnp.stack(priors)
    raw_scores = jnp.einsum(
        "bthd,bshd->bhts", query_blk, key_blk, preferred_element_type=jnp.float32
    )
    scores = (raw_scores * decay_mask[None]).astype(jnp.bfloat16)
    intra = jnp.einsum("bhts,bshd->bthd", scores, value_blk, preferred_element_type=jnp.float32)
    inter = precise("bthd,bhde->bthe", query_decay, prior_states)
    mixed = (intra + inter).reshape(tok_rows, width)
    mixed_norm = rms_norm(mixed)
    gated = (mixed_norm * gate_rows).astype(jnp.bfloat16)
    stream = residual_in + matmul(gated, attn_full[4])
    normed_mid = rms_norm(stream).astype(jnp.bfloat16)
    left_pre = matmul(normed_mid, ffn_full[0])
    right_pre = matmul(normed_mid, ffn_full[1])
    product = (left_pre * right_pre).astype(jnp.bfloat16)
    output = (token_mask[:, None] * (stream + matmul(product, ffn_full[2]))).astype(jnp.bfloat16)
    grad_rows = cotangent[0].astype(jnp.float32) * token_mask[:, None]
    grad_low = grad_rows.astype(jnp.bfloat16)
    ffn_back = ffn_full
    grad_product = matmul_right_t(grad_low, ffn_back[2])
    grad_left = (grad_product * right_pre).astype(jnp.bfloat16)
    grad_right = (grad_product * left_pre).astype(jnp.bfloat16)
    term_down = matmul_left_t(product, grad_low)
    term_left = matmul_left_t(normed_mid, grad_left)
    term_right = matmul_left_t(normed_mid, grad_right)
    grad_mid = matmul_right_t(grad_left, ffn_back[0]) + matmul_right_t(grad_right, ffn_back[1])
    ffn_terms = jnp.concatenate((term_left, term_right, term_down.reshape(width, hidden)), axis=1)
    ffn_sum = lax.psum_scatter(ffn_terms.astype(jnp.bfloat16), ("seq", "fsdp"), scatter_dimension=0, tiled=True)
    ffn_grads = (
        ffn_sum[:, :hidden].astype(jnp.float32),
        ffn_sum[:, hidden : 2 * hidden].astype(jnp.float32),
        ffn_sum[:, 2 * hidden :].reshape(w_down.shape).astype(jnp.float32),
    )
    grad_stream = grad_rows + norm_back(stream, grad_mid)
    grad_stream_low = grad_stream.astype(jnp.bfloat16)
    attn_back = attn_full
    term_out = matmul_left_t(gated, grad_stream_low)
    grad_gated = matmul_right_t(grad_stream_low, attn_back[4])
    grad_gate_rows = grad_gated * mixed_norm
    grad_mixed = norm_back(mixed, grad_gated * gate_rows)
    grad_mix_blk = grad_mixed.astype(jnp.bfloat16).reshape(shape_four)
    grad_mix_full = grad_mix_blk.astype(jnp.float32)
    grad_scores = jnp.einsum(
        "bthe,bshe->bhts", grad_mix_blk, value_blk, preferred_element_type=jnp.float32
    )
    grad_raw = (grad_scores * decay_mask[None]).astype(jnp.bfloat16)
    grad_prior = precise("bthd,bthe->bhde", query_decay, grad_mix_full)
    back_state = identity[1]
    for number in reversed(range(blocks)):
        back_state = keep_state[number] * (
            grad_prior[number] + decay_block[:, None, None] * back_state
        )
    arriving = carried_in((carry_scale, back_state), "seq", affine_join, identity)
    later_grad = arriving[1]
    state_list = [later_grad] * blocks
    for number in reversed(range(blocks)):
        state_list[number] = later_grad
        later_grad = keep_state[number] * (
            grad_prior[number] + decay_block[:, None, None] * later_grad
        )
    state_grads = jnp.stack(state_list)
    query_grad = jnp.einsum(
        "bhts,bshd->bthd", grad_raw, key_blk, preferred_element_type=jnp.float32
    )
    query_grad = query_grad + decay_in[None, :, :, None] * precise(
        "bthe,bhde->bthd", grad_mix_full, prior_states
    )
    key_grad = jnp.einsum(
        "bhts,bthd->bshd", grad_raw, query_blk, preferred_element_type=jnp.float32
    )
    key_grad = key_grad + decay_out[None, :, :, None] * precise(
        "bthe,bhde->bthd", value_full, state_grads
    )
    value_grad = jnp.einsum(
        "bhts,bthe->bshe", scores, grad_mix_blk, preferred_element_type=jnp.float32
    )
    value_grad = value_grad + decay_out[None, :, :, None] * precise(
        "bthd,bhde->bthe", key_full, state_grads
    )
    grad_query_pre = (query_grad.reshape(tok_rows, width) * silu_slope(query_pre)).astype(
        jnp.bfloat16
    )
    grad_key_pre = (
        key_grad.reshape(tok_rows, width) * token_mask[:, None] * silu_slope(key_pre)
    ).astype(jnp.bfloat16)
    grad_value_pre = (value_grad.reshape(tok_rows, width) * silu_slope(value_pre)).astype(
        jnp.bfloat16
    )
    grad_gate_pre = (grad_gate_rows * silu_slope(gate_pre)).astype(jnp.bfloat16)
    term_query = matmul_left_t(normed_in, grad_query_pre)
    term_key = matmul_left_t(normed_in, grad_key_pre)
    term_value = matmul_left_t(normed_in, grad_value_pre)
    term_gate = matmul_left_t(normed_in, grad_gate_pre)
    grad_normed = matmul_right_t(grad_query_pre, attn_back[0]) + matmul_right_t(
        grad_key_pre, attn_back[1]
    )
    grad_normed = (
        grad_normed
        + matmul_right_t(grad_value_pre, attn_back[2])
        + matmul_right_t(grad_gate_pre, attn_back[3])
    )
    attn_terms = jnp.concatenate((term_query, term_key, term_value, term_gate, term_out), axis=1)
    attn_sum = lax.psum_scatter(attn_terms.astype(jnp.bfloat16), ("seq", "fsdp"), scatter_dimension=0, tiled=True)
    attn_grads = tuple(attn_sum[:, n * width : (n + 1) * width].astype(jnp.float32) for n in range(5))
    grad_input = grad_stream + norm_back(residual_in, grad_normed)
    return (
        output[None],
        grad_input[None],
        attn_grads[0],
        attn_grads[1],
        attn_grads[2],
        attn_grads[3],
        attn_grads[4],
        ffn_grads[0],
        ffn_grads[1],
        ffn_grads[2],
    )


def solution(mesh):
    return jax.shard_map(
        on_device,
        mesh=mesh,
        in_specs=(
            P("fsdp", "seq", None),
            P("fsdp", "seq"),
            P("fsdp", "seq"),
            P(),
            P(("seq", "fsdp"), None),
            P(("seq", "fsdp"), None),
            P(("seq", "fsdp"), None),
            P(("seq", "fsdp"), None),
            P(("seq", "fsdp"), None),
            P(("seq", "fsdp"), None),
            P(("seq", "fsdp"), None),
            P(("seq", "fsdp"), None),
            P("fsdp", "seq", None),
        ),
        out_specs=(
            P("fsdp", "seq", None),
            P("fsdp", "seq", None),
            P(("seq", "fsdp"), None),
            P(("seq", "fsdp"), None),
            P(("seq", "fsdp"), None),
            P(("seq", "fsdp"), None),
            P(("seq", "fsdp"), None),
            P(("seq", "fsdp"), None),
            P(("seq", "fsdp"), None),
            P(("seq", "fsdp"), None),
        ),
        check_vma=False,
    )
```

```python
import functools

import jax
import jax.numpy as jnp
from jax import lax
from jax.experimental import pallas as pl
from jax.experimental.pallas import tpu as pltpu
from jax.sharding import PartitionSpec as P

MESH = pl.DeviceIdType.MESH
bf = jnp.bfloat16
f32 = jnp.float32
Z, Y, X, C = 4, 2, 2, 2
def half(rows):
    a=(rows//2+7)//8*8
    return (pl.ds(0,a),a),(pl.ds(a,rows-a),rows-a)
def ag_kernel(*refs, nw):
    chunks=refs[:nw]; fulls=refs[nw:2*nw]
    (lsem,zs,zr,as_,ar,bs,br,as3,ar3,bs3,br3,cs,cr)=refs[2*nw:]
    s=lax.axis_index("seq"); f=lax.axis_index("fsdp")
    z=s//Y; y=s%Y; x=f//C; c=f%C
    def dev(zz,yy,xx,cc): return (zz*Y+yy, xx*C+cc)
    xp=dev(z,y,1-x,c); yp=dev(z,1-y,x,c); cp=dev(z,y,x,1-c)
    zps=[(z+k)%Z for k in range(1,Z)]
    bar=pltpu.get_barrier_semaphore()
    for d in [xp,yp,cp]+[dev(q,y,x,c) for q in zps]:
        pl.semaphore_signal(bar,inc=1,device_id=d,device_id_type=MESH)
    pl.semaphore_wait(bar,6)
    def rc(src,dst,ss,rs,d): return pltpu.make_async_remote_copy(src_ref=src,dst_ref=dst,send_sem=ss,recv_sem=rs,device_id=d,device_id_type=MESH)
    desc={}
    def start(key,*a):
        r=rc(*a); r.start(); desc.setdefault(key,[]).append(r)
    for w in range(nw):
        F=fulls[w]
        lc=pltpu.make_async_copy(chunks[w],F.at[z,y,x,c],lsem.at[w]); lc.start(); desc[("l",w)]=[lc]
        for q in zps:
            start(("z",w),chunks[w],F.at[z,y,x,c],zs.at[w],zr.at[w],dev(q,y,x,c))
    def wait_recv(n_ref,sem):
        pltpu.make_async_copy(n_ref,n_ref,sem).wait()
    def s2(w):
        F=fulls[w]; (A,na),(B,nb)=half(F.shape[4])
        desc[("l",w)][0].wait()
        wait_recv(F.at[pl.ds(0,3),y,x,c],zr.at[w])
        start(("a",w),F.at[:,y,x,c,A],F.at[:,y,x,c,A],as_.at[w],ar.at[w],xp)
        start(("b",w),F.at[:,y,x,c,B],F.at[:,y,x,c,B],bs.at[w],br.at[w],yp)
        start(("c",w),F.at[:,y,x,c],F.at[:,y,x,c],cs.at[w],cr.at[w],cp)
    def s3(w):
        F=fulls[w]; (A,na),(B,nb)=half(F.shape[4])
        wait_recv(F.at[:,y,1-x,c,A],ar.at[w])
        start(("a3",w),F.at[:,y,:,c,A],F.at[:,y,:,c,A],as3.at[w],ar3.at[w],yp)
        start(("c",w),F.at[:,y,1-x,c,A],F.at[:,y,1-x,c,A],cs.at[w],cr.at[w],cp)
        wait_recv(F.at[:,1-y,x,c,B],br.at[w])
        start(("b3",w),F.at[:,:,x,c,B],F.at[:,:,x,c,B],bs3.at[w],br3.at[w],xp)
        start(("c",w),F.at[:,1-y,x,c,B],F.at[:,1-y,x,c,B],cs.at[w],cr.at[w],cp)
    def s4(w):
        F=fulls[w]; (A,na),(B,nb)=half(F.shape[4])
        wait_recv(F.at[:,1-y,:,c,A],ar3.at[w])
        start(("c",w),F.at[:,1-y,:,c,A],F.at[:,1-y,:,c,A],cs.at[w],cr.at[w],cp)
        wait_recv(F.at[:,:,1-x,c,B],br3.at[w])
        start(("c",w),F.at[:,:,1-x,c,B],F.at[:,:,1-x,c,B],cs.at[w],cr.at[w],cp)
    def s5(w):
        F=fulls[w]
        wait_recv(F.at[:,:,:,1-c],cr.at[w])
    for t in range(nw+3):
        if t<nw: s2(t)
        if 0<=t-1<nw: s3(t-1)
        if 0<=t-2<nw: s4(t-2)
        if 0<=t-3<nw: s5(t-3)
    for k,v in desc.items():
        if k[0]!="l":
            for r in v: r.wait_send()
def ag(chunks, space=pl.ANY):
    nw=len(chunks)
    out=[jax.ShapeDtypeStruct((Z,Y,X,C)+c.shape,c.dtype) for c in chunks]
    D=pltpu.SemaphoreType.DMA((nw,))
    return pl.pallas_call(functools.partial(ag_kernel,nw=nw),out_shape=out,
      in_specs=[pl.BlockSpec(memory_space=pl.ANY)]*nw,out_specs=[pl.BlockSpec(memory_space=space)]*nw,
      scratch_shapes=[D]*13,compiler_params=pltpu.CompilerParams(collective_id=0,has_side_effects=True,vmem_limit_bytes=63<<20))(*chunks)
def rs_kernel(*refs, nw):
    src=refs[:nw]; outs=refs[nw:2*nw]; rcs=refs[2*nw:3*nw]; r3a=refs[3*nw:4*nw]; r3b=refs[4*nw:5*nw]; r2a=refs[5*nw:6*nw]; r2b=refs[6*nw:7*nw]; rz=refs[7*nw:8*nw]
    T=refs[8*nw:9*nw]; st=refs[9*nw:9*nw+3]; fo=refs[9*nw+3:9*nw+6]
    (lsem,osem,stsem,ss,rsem)=refs[9*nw+6:]
    s=lax.axis_index("seq"); f=lax.axis_index("fsdp")
    z=s//Y; y=s%Y; x=f//C; c=f%C
    def dev(zz,yy,xx,cc): return (zz*Y+yy, xx*C+cc)
    xp=dev(z,y,1-x,c); yp=dev(z,1-y,x,c); cp=dev(z,y,x,1-c)
    zps=[(z+k)%Z for k in range(1,Z)]
    bar=pltpu.get_barrier_semaphore()
    for d in [xp,yp,cp]+[dev(q,y,x,c) for q in zps]:
        pl.semaphore_signal(bar,inc=1,device_id=d,device_id_type=MESH)
    pl.semaphore_wait(bar,6)
    sends=[]
    def start(w,k,src,dst,d):
        r=pltpu.make_async_remote_copy(src_ref=src,dst_ref=dst,send_sem=ss.at[w,k],recv_sem=rsem.at[w,k],device_id=d,device_id_type=MESH)
        r.start(); sends.append(r)
    def wait_recv(w,k,ref): pltpu.make_async_copy(ref,ref,rsem.at[w,k]).wait()
    def kind(w):
        return 0 if T[w].shape[4:]==(32,1024) else (1 if T[w].shape[4:]==(32,2816) else 2)
    def add(w, recv, dstf, rows):
        n=recv.shape[1]; S=st[kind(w)]; R=recv.shape[2]
        def cpy(zz,slot): return pltpu.make_async_copy(recv.at[zz],S.at[slot,pl.ds(0,n),pl.ds(0,R)],stsem.at[slot])
        cpy(0,0).start()
        def body(zz,_):
            slot=zz%2
            @pl.when(zz+1<Z)
            def _(): cpy(zz+1,1-slot).start()
            cpy(zz,slot).wait()
            for i in range(n):
                d=dstf(zz,i)
                d[...]=(d[...].astype(f32)+S[slot,i,pl.ds(0,R)].astype(f32)).astype(bf)
            return 0
        lax.fori_loop(0,Z,body,0)
    def L(w):
        r=pltpu.make_async_copy(src[w],T[w],lsem.at[w]); return r
    for w in range(nw): L(w).start()
    def c0(w):
        L(w).wait()
        start(w,0,T[w].at[:,:,:,1-c],rcs[w],cp)
    def c1(w):
        t=T[w]; (A,na),(B,nb)=half(t.shape[4])
        wait_recv(w,0,rcs[w])
        add4(w)
        start(w,1,t.at[:,1-y,:,c,A],r3a[w],yp)
        start(w,2,t.at[:,:,1-x,c,B],r3b[w],xp)
    def add4(w):
        t=T[w]; S=st[kind(w)]
        def cpy(zz,slot): return pltpu.make_async_copy(rcs[w].at[zz],S.at[slot],stsem.at[slot])
        cpy(0,0).start()
        def body(zz,_):
            slot=zz%2
            @pl.when(zz+1<Z)
            def _(): cpy(zz+1,1-slot).start()
            cpy(zz,slot).wait()
            for yy in range(Y):
                for xx in range(X):
                    d=t.at[zz,yy,xx,c]
                    d[...]=(d[...].astype(f32)+S[slot,yy,xx].astype(f32)).astype(bf)
            return 0
        lax.fori_loop(0,Z,body,0)
    def add2(w,recv,dstf):
        S=st[kind(w)]; R=recv.shape[2]
        def cpy(zz,slot): return pltpu.make_async_copy(recv.at[zz],S.at[slot,0,:,pl.ds(0,R)],stsem.at[slot])
        cpy(0,0).start()
        def body(zz,_):
            slot=zz%2
            @pl.when(zz+1<Z)
            def _(): cpy(zz+1,1-slot).start()
            cpy(zz,slot).wait()
            for i in range(2):
                d=dstf(zz,i)
                d[...]=(d[...].astype(f32)+S[slot,0,i,pl.ds(0,R)].astype(f32)).astype(bf)
            return 0
        lax.fori_loop(0,Z,body,0)
    def add1(w,recv,dstf):
        S=st[kind(w)]; R=recv.shape[1]
        def cpy(zz,slot): return pltpu.make_async_copy(recv.at[zz],S.at[slot,0,0,pl.ds(0,R)],stsem.at[slot])
        cpy(0,0).start()
        def body(zz,_):
            slot=zz%2
            @pl.when(zz+1<Z)
            def _(): cpy(zz+1,1-slot).start()
            cpy(zz,slot).wait()
            d=dstf(zz)
            d[...]=(d[...].astype(f32)+S[slot,0,0,pl.ds(0,R)].astype(f32)).astype(bf)
            return 0
        lax.fori_loop(0,Z,body,0)
    def c2(w):
        t=T[w]; (A,na),(B,nb)=half(t.shape[4])
        wait_recv(w,1,r3a[w]); add2(w,r3a[w],lambda zz,i: t.at[zz,y,i,c,A])
        start(w,3,t.at[:,y,1-x,c,A],r2a[w],xp)
        wait_recv(w,2,r3b[w]); add2(w,r3b[w],lambda zz,i: t.at[zz,i,x,c,B])
        start(w,4,t.at[:,1-y,x,c,B],r2b[w],yp)
    def c3(w):
        t=T[w]; (A,na),(B,nb)=half(t.shape[4])
        wait_recv(w,3,r2a[w]); add1(w,r2a[w],lambda zz: t.at[zz,y,x,c,A])
        wait_recv(w,4,r2b[w]); add1(w,r2b[w],lambda zz: t.at[zz,y,x,c,B])
        for k in range(1,Z):
            start(w,5,t.at[(z+k)%Z,y,x,c],rz[w].at[k-1],dev((z+k)%Z,y,x,c))
    def c4(w):
        t=T[w]; S=st[kind(w)]; O=fo[kind(w)]
        wait_recv(w,5,rz[w])
        S3=S.at[0].at[0]
        cps=[pltpu.make_async_copy(rz[w].at[k],S.at[k//2,0,k%2],stsem.at[k//2]) for k in range(Z-1)]
        for q in cps: q.start()
        for q in cps: q.wait()
        v=t[z,y,x,c].astype(f32)
        for k in range(Z-1): v=v+S[k//2,0,k%2].astype(f32)
        O[...]=v
        o=pltpu.make_async_copy(O,outs[w],osem); o.start(); o.wait()
    for t_ in range(nw+4):
        for i,fn in enumerate((c0,c1,c2,c3,c4)):
            if 0<=t_-i<nw: fn(t_-i)
    for r in sends: r.wait_send()
def rs(terms):
    nw=len(terms); S=jax.ShapeDtypeStruct
    cs=[t.shape[4:] for t in terms]
    hb=lambda r:((r//2+7)//8*8, r-(r//2+7)//8*8)
    out=[S(c,f32) for c in cs]+[S((Z,Y,X)+c,bf) for c in cs]+[S((Z,X,hb(c[0])[0],c[1]),bf) for c in cs]+[S((Z,Y,hb(c[0])[1],c[1]),bf) for c in cs]\
      +[S((Z,hb(c[0])[0],c[1]),bf) for c in cs]+[S((Z,hb(c[0])[1],c[1]),bf) for c in cs]+[S((Z-1,)+c,bf) for c in cs]
    kinds=[(32,1024),(32,2816),(88,1024)]
    scr=[pltpu.VMEM(t.shape,bf) for t in terms]+[pltpu.VMEM((2,Y,X)+k,bf) for k in kinds]+[pltpu.VMEM(k,f32) for k in kinds]
    D=pltpu.SemaphoreType.DMA
    scr+=[D((nw,)),D,D((2,)),D((nw,6)),D((nw,6))]
    A=pl.BlockSpec(memory_space=pl.ANY)
    return pl.pallas_call(functools.partial(rs_kernel,nw=nw),out_shape=out,in_specs=[A]*nw,out_specs=[A]*len(out),scratch_shapes=scr,
       compiler_params=pltpu.CompilerParams(collective_id=1,has_side_effects=True,vmem_limit_bytes=63<<20))(*terms)[:nw]

EPSILON = 1e-06
HIGHEST = lax.Precision.HIGHEST


def entering(value, axis, join, neutral):
    count, mine = (lax.axis_size(axis), lax.axis_index(axis))
    pieces = jax.tree.map(lambda part: lax.all_gather(part, axis), value)
    running = jax.tree.map(
        lambda part, zero: jnp.full_like(part, 0) + jnp.asarray(zero, part.dtype), value, neutral
    )

    def hop(position, running):
        longer = join(running, jax.tree.map(lambda part: part[position], pieces))
        return jax.tree.map(lambda new, old: jnp.where(position < mine, new, old), longer, running)

    return lax.fori_loop(0, count - 1, hop, running)


def carried_in(x, axis, join, neutral):
    count = lax.axis_size(axis)
    place = lax.axis_index(axis)
    ahead = count - 1 - place
    gathered = jax.tree.map(
        lambda a, kind: lax.all_gather(a.astype(kind), axis), x, (jnp.bfloat16, jnp.bfloat16)
    )
    state = jax.tree.map(lambda a, e: jnp.zeros_like(a) + jnp.asarray(e, a.dtype), x, neutral)

    def one(hop, state):
        source = count - 1 - hop
        return join(
            state,
            jax.tree.map(
                lambda a, own: lax.dynamic_index_in_dim(a, source, 0, False).astype(own.dtype),
                gathered,
                x,
            ),
        )

    return lax.fori_loop(0, ahead, one, state)


def rms_norm(values):
    return values * lax.rsqrt(jnp.mean(values * values, axis=-1, keepdims=True) + EPSILON)


def norm_back(values, grad_norm):
    _, pull = jax.vjp(rms_norm, values)
    return pull(grad_norm)[0]


def silu_slope(values):
    sigma = jax.nn.sigmoid(values)
    return sigma * (1.0 + values * (1.0 - sigma))


def affine_join(earlier, later):
    return (earlier[0] * later[0], later[0][:, None, None] * earlier[1] + later[1])


def matmul(left, right):
    return jnp.dot(left, right, preferred_element_type=jnp.float32)


def matmul_left_t(left, right):
    return jnp.einsum("ab,ac->bc", left, right, preferred_element_type=jnp.float32)


def matmul_right_t(left, right):
    return jnp.einsum("ab,cb->ac", left, right, preferred_element_type=jnp.float32)


def precise(form, left, right):
    return jnp.einsum(form, left, right, precision=HIGHEST)


def fits(w_query, w_down):
    shape = (lax.axis_size("seq"), lax.axis_size("fsdp"))
    return shape == (Z * Y, X * C) and w_query.shape[0] % 16 == 0 and w_down.shape[0] % 8 == 0


def on_device(
    hidden_in,
    block_counts,
    seq_starts,
    decay_rates,
    w_query,
    w_key,
    w_value,
    w_gate,
    w_out,
    w_left,
    w_right,
    w_down,
    cotangent,
):
    tok_rows = hidden_in.shape[1]
    width = hidden_in.shape[2]
    heads = decay_rates.shape[0]
    head_dim = width // heads
    blocks = block_counts.shape[1]
    block_len = tok_rows // blocks
    residual_in = hidden_in[0].astype(jnp.float32)
    offsets = jnp.arange(block_len)
    token_mask = (offsets[None, :] < block_counts[0][:, None]).astype(jnp.float32).reshape(tok_rows)
    keep_state = (1 - seq_starts[0]).astype(jnp.float32)
    position = offsets.astype(jnp.float32)
    decay_in = jnp.exp(-(position[:, None] + 1.0) * decay_rates[None, :])
    decay_out = jnp.exp(-(block_len - 1.0 - position[:, None]) * decay_rates[None, :])
    decay_block = jnp.exp(-block_len * decay_rates)
    distance = position[:, None] - position[None, :]
    decay_mask = jnp.where(
        distance[None] >= 0,
        jnp.exp(-jnp.maximum(distance, 0.0)[None] * decay_rates[:, None, None]),
        0.0,
    )
    shape_four = (blocks, block_len, heads, head_dim)
    identity = (
        jnp.ones((heads,), jnp.float32),
        jnp.zeros((heads, head_dim, head_dim), jnp.float32),
    )
    own = (w_query, w_key, w_value, w_gate, w_out, w_left, w_right, w_down)
    kernels = fits(w_query, w_down)
    hidden = w_left.shape[1]
    if kernels:
        whole = [part.reshape(-1, part.shape[-1]) for part in ag(own)]
        attn_full = tuple(whole[:5])
        ffn_full = tuple(whole[5:])
    else:
        rows = w_query.shape[0]
        packed = jnp.concatenate(
            (w_query, w_key, w_value, w_gate, w_out, w_left, w_right, w_down.reshape(rows, hidden)),
            axis=1,
        )
        full = lax.all_gather(packed, ("seq", "fsdp"), axis=0, tiled=True)
        attn_full = tuple(full[:, n * width : (n + 1) * width] for n in range(5))
        ffn_full = (
            full[:, 5 * width : 5 * width + hidden],
            full[:, 5 * width + hidden : 5 * width + 2 * hidden],
            full[:, 5 * width + 2 * hidden :].reshape(hidden, width),
        )
    normed_in = rms_norm(residual_in).astype(jnp.bfloat16)
    query_pre = matmul(normed_in, attn_full[0])
    key_pre = matmul(normed_in, attn_full[1])
    value_pre = matmul(normed_in, attn_full[2])
    gate_pre = matmul(normed_in, attn_full[3])
    query_rows = jax.nn.silu(query_pre).astype(jnp.bfloat16)
    key_rows = (jax.nn.silu(key_pre) * token_mask[:, None]).astype(jnp.bfloat16)
    value_rows = jax.nn.silu(value_pre).astype(jnp.bfloat16)
    gate_rows = jax.nn.silu(gate_pre)
    query_blk = query_rows.reshape(shape_four)
    key_blk = key_rows.reshape(shape_four)
    value_blk = value_rows.reshape(shape_four)
    key_full = key_blk.astype(jnp.float32)
    value_full = value_blk.astype(jnp.float32)
    query_decay = query_blk.astype(jnp.float32) * decay_in[None, :, :, None]
    key_decay = key_full * decay_out[None, :, :, None]
    local_states = precise("bthd,bthe->bhde", key_decay, value_full)
    carry_scale = identity[0]
    carry_state = identity[1]
    number = 0
    factor = keep_state[number] * decay_block
    carry_scale = carry_scale * factor
    carry_state = factor[:, None, None] * carry_state + local_states[number]
    arrived = entering((carry_scale, carry_state), "seq", affine_join, identity)
    state_now = arrived[1]
    number = 0
    prior = keep_state[number] * state_now
    priors = [prior]
    prior_states = jnp.stack(priors)
    raw_scores = jnp.einsum(
        "bthd,bshd->bhts", query_blk, key_blk, preferred_element_type=jnp.float32
    )
    scores = (raw_scores * decay_mask[None]).astype(jnp.bfloat16)
    intra = jnp.einsum("bhts,bshd->bthd", scores, value_blk, preferred_element_type=jnp.float32)
    inter = precise("bthd,bhde->bthe", query_decay, prior_states)
    mixed = (intra + inter).reshape(tok_rows, width)
    mixed_norm = rms_norm(mixed)
    gated = (mixed_norm * gate_rows).astype(jnp.bfloat16)
    stream = residual_in + matmul(gated, attn_full[4])
    normed_mid = rms_norm(stream).astype(jnp.bfloat16)
    left_pre = matmul(normed_mid, ffn_full[0])
    right_pre = matmul(normed_mid, ffn_full[1])
    product = (left_pre * right_pre).astype(jnp.bfloat16)
    output = (token_mask[:, None] * (stream + matmul(product, ffn_full[2]))).astype(jnp.bfloat16)
    grad_rows = cotangent[0].astype(jnp.float32) * token_mask[:, None]
    grad_low = grad_rows.astype(jnp.bfloat16)
    ffn_back = ffn_full
    grad_product = matmul_right_t(grad_low, ffn_back[2])
    grad_left = (grad_product * right_pre).astype(jnp.bfloat16)
    grad_right = (grad_product * left_pre).astype(jnp.bfloat16)
    term_down = matmul_left_t(product, grad_low)
    term_left = matmul_left_t(normed_mid, grad_left)
    term_right = matmul_left_t(normed_mid, grad_right)
    grad_mid = matmul_right_t(grad_left, ffn_back[0]) + matmul_right_t(grad_right, ffn_back[1])
    grad_stream = grad_rows + norm_back(stream, grad_mid)
    grad_stream_low = grad_stream.astype(jnp.bfloat16)
    attn_back = attn_full
    term_out = matmul_left_t(gated, grad_stream_low)
    grad_gated = matmul_right_t(grad_stream_low, attn_back[4])
    grad_gate_rows = grad_gated * mixed_norm
    grad_mixed = norm_back(mixed, grad_gated * gate_rows)
    grad_mix_blk = grad_mixed.astype(jnp.bfloat16).reshape(shape_four)
    grad_mix_full = grad_mix_blk.astype(jnp.float32)
    grad_scores = jnp.einsum(
        "bthe,bshe->bhts", grad_mix_blk, value_blk, preferred_element_type=jnp.float32
    )
    grad_raw = (grad_scores * decay_mask[None]).astype(jnp.bfloat16)
    grad_prior = precise("bthd,bthe->bhde", query_decay, grad_mix_full)
    back_state = identity[1]
    for number in reversed(range(blocks)):
        back_state = keep_state[number] * (
            grad_prior[number] + decay_block[:, None, None] * back_state
        )
    arriving = carried_in((carry_scale, back_state), "seq", affine_join, identity)
    later_grad = arriving[1]
    state_list = [later_grad] * blocks
    for number in reversed(range(blocks)):
        state_list[number] = later_grad
        later_grad = keep_state[number] * (
            grad_prior[number] + decay_block[:, None, None] * later_grad
        )
    state_grads = jnp.stack(state_list)
    query_grad = jnp.einsum(
        "bhts,bshd->bthd", grad_raw, key_blk, preferred_element_type=jnp.float32
    )
    query_grad = query_grad + decay_in[None, :, :, None] * precise(
        "bthe,bhde->bthd", grad_mix_full, prior_states
    )
    key_grad = jnp.einsum(
        "bhts,bthd->bshd", grad_raw, query_blk, preferred_element_type=jnp.float32
    )
    key_grad = key_grad + decay_out[None, :, :, None] * precise(
        "bthe,bhde->bthd", value_full, state_grads
    )
    value_grad = jnp.einsum(
        "bhts,bthe->bshe", scores, grad_mix_blk, preferred_element_type=jnp.float32
    )
    value_grad = value_grad + decay_out[None, :, :, None] * precise(
        "bthd,bhde->bthe", key_full, state_grads
    )
    grad_query_pre = (query_grad.reshape(tok_rows, width) * silu_slope(query_pre)).astype(
        jnp.bfloat16
    )
    grad_key_pre = (
        key_grad.reshape(tok_rows, width) * token_mask[:, None] * silu_slope(key_pre)
    ).astype(jnp.bfloat16)
    grad_value_pre = (value_grad.reshape(tok_rows, width) * silu_slope(value_pre)).astype(
        jnp.bfloat16
    )
    grad_gate_pre = (grad_gate_rows * silu_slope(gate_pre)).astype(jnp.bfloat16)
    term_query = matmul_left_t(normed_in, grad_query_pre)
    term_key = matmul_left_t(normed_in, grad_key_pre)
    term_value = matmul_left_t(normed_in, grad_value_pre)
    term_gate = matmul_left_t(normed_in, grad_gate_pre)
    grad_normed = matmul_right_t(grad_query_pre, attn_back[0]) + matmul_right_t(
        grad_key_pre, attn_back[1]
    )
    grad_normed = (
        grad_normed
        + matmul_right_t(grad_value_pre, attn_back[2])
        + matmul_right_t(grad_gate_pre, attn_back[3])
    )
    if kernels:
        terms = (term_down, term_left, term_right, term_out, term_gate, term_value, term_key, term_query)
        split = [t.astype(bf).reshape((Z, Y, X, C, t.shape[0] // (Z * Y * X * C), t.shape[1])) for t in terms]
        sums = rs(split)
        attn_grads = (sums[7], sums[6], sums[5], sums[4], sums[3])
        ffn_grads = (sums[1], sums[2], sums[0])
    else:
        ffn_grads = (
            lax.psum_scatter(term_left, ("seq", "fsdp"), scatter_dimension=0, tiled=True),
            lax.psum_scatter(term_right, ("seq", "fsdp"), scatter_dimension=0, tiled=True),
            lax.psum_scatter(term_down, ("seq", "fsdp"), scatter_dimension=0, tiled=True),
        )
        attn_grads = (
            lax.psum_scatter(term_query, ("seq", "fsdp"), scatter_dimension=0, tiled=True),
            lax.psum_scatter(term_key, ("seq", "fsdp"), scatter_dimension=0, tiled=True),
            lax.psum_scatter(term_value, ("seq", "fsdp"), scatter_dimension=0, tiled=True),
            lax.psum_scatter(term_gate, ("seq", "fsdp"), scatter_dimension=0, tiled=True),
            lax.psum_scatter(term_out, ("seq", "fsdp"), scatter_dimension=0, tiled=True),
        )
    grad_input = grad_stream + norm_back(residual_in, grad_normed)
    return (
        output[None],
        grad_input[None],
        attn_grads[0],
        attn_grads[1],
        attn_grads[2],
        attn_grads[3],
        attn_grads[4],
        ffn_grads[0],
        ffn_grads[1],
        ffn_grads[2],
    )


def solution(mesh):
    return jax.shard_map(
        on_device,
        mesh=mesh,
        in_specs=(
            P("fsdp", "seq", None),
            P("fsdp", "seq"),
            P("fsdp", "seq"),
            P(),
            P(("seq", "fsdp"), None),
            P(("seq", "fsdp"), None),
            P(("seq", "fsdp"), None),
            P(("seq", "fsdp"), None),
            P(("seq", "fsdp"), None),
            P(("seq", "fsdp"), None),
            P(("seq", "fsdp"), None),
            P(("seq", "fsdp"), None),
            P("fsdp", "seq", None),
        ),
        out_specs=(
            P("fsdp", "seq", None),
            P("fsdp", "seq", None),
            P(("seq", "fsdp"), None),
            P(("seq", "fsdp"), None),
            P(("seq", "fsdp"), None),
            P(("seq", "fsdp"), None),
            P(("seq", "fsdp"), None),
            P(("seq", "fsdp"), None),
            P(("seq", "fsdp"), None),
            P(("seq", "fsdp"), None),
        ),
        check_vma=False,
    )
```

```python
import functools

import jax
import jax.numpy as jnp
from jax import lax
from jax.experimental import pallas as pl
from jax.experimental.pallas import tpu as pltpu
from jax.sharding import PartitionSpec as P

MESH = pl.DeviceIdType.MESH
BF = jnp.bfloat16
F32 = jnp.float32
EPS = 1e-06
Z, Y, X, C = 4, 2, 2, 2
SEQ, FSDP = Z * Y, X * C
TILE = 256
NT = (((1,), (1,)), ((), ()))
TN = (((0,), (0,)), ((), ()))

PARTS = (4, 4, 3)
ORDER = (
    "g0:q", "g0:k", "g0:v", "g1:q", "g2a:q", "g1:k", "g0:g", "g0:r0", "g1:v", "g2b:q", "g2a:k", "g0:d0", "g2b:v",
    "g1:g", "g3b:q", "prepare", "g0:l0", "g0:o", "g3a:k", "g2a:v", "g0:l1", "g1:r0", "g1:d0", "g3a:v", "g2a:g",
    "g2b:k", "g2a:r0", "g3b:v", "g2b:d0", "g4:v", "g1:l1", "g3b:k", "g2a:d0", "g2b:g", "project:v", "g1:l0", "g4:k",
    "project:k", "g0:r2", "g1:o", "g2b:r0", "g0:d1", "g3a:g", "g3a:r0", "local_state", "g0:l2", "g3b:g", "pair:1",
    "g2b:l1", "g2a:l0", "g1:d1", "g2b:o", "g2b:l0", "g2a:o", "g3a:q", "g4:q", "B:1", "g2b:d1", "g3b:r0", "g2a:d1",
    "C:1", "g3a:o", "g2a:l1", "g0:r1", "g3b:o", "g3a:l0", "g4:g", "project:q", "local_mix", "g3b:d0", "project:g",
    "g1:l2", "fin:1", "g3b:l0", "g3a:d1", "g3a:d0", "g1:r1", "g4:r0", "g3a:l1", "add_prior", "g4:l0", "g3b:d1",
    "g4:d0", "gate", "g3b:l1", "g1:r2", "g4:o", "to_stream", "g2b:r1", "g4:d1", "g4:l1", "g2a:r1", "ffn:0", "g2a:r2",
    "term:l0", "ffn_out:0", "s0:l0", "g3b:r1", "g2b:l2", "term:r0", "g3a:r1", "g2a:l2", "term_d:0", "g2b:r2", "s0:r0",
    "s1:l0", "g4:r1", "ffn:1", "term:r1", "s0:r1", "s1:r0", "ffn_out:1", "g3a:r2", "g3a:l2", "g3b:l2", "g3b:r2",
    "term:l1", "term_d:1", "s1:r1", "g4:r2", "s2b:l0", "g4:l2", "ffn:2", "s2b:r0", "s0:l1", "term:l2", "s2a:l0",
    "ffn_out:2", "finish_out", "term_d:2", "s1:l1", "s0:l2", "to_grad_stream", "back_gated", "s1:l2", "s0:d0",
    "s2a:r1", "term:r2", "term:o", "s0:r2", "back_gate", "s0:d1", "back_scores", "bn:g", "pair:-1", "s3:l0", "s1:d0",
    "s1:r2", "s0:o", "s2b:l1", "B:-1", "s2a:r0", "s2a:l2", "s4:l0", "s2a:l1", "back_query", "C:-1", "bn:q", "s2b:r1",
    "s1:o", "term:q", "s2a:r2", "s2b:r2", "s3:r1", "s1:d1", "s2b:o", "s3:r0", "s2b:l2", "fin:-1", "s0:q", "s3:l1",
    "back_kv", "s3:r2", "s2a:d0", "term:g", "s2a:o", "s1:q", "bn:k", "bn:v", "term:k", "s2a:d1", "s2b:d1", "s3:l2",
    "s0:g", "term:v", "s0:k", "s4:r0", "s3:o", "s1:g", "finish_grad", "s2b:d0", "s0:v", "s2b:q", "s4:r1", "s2a:q",
    "s3:d1", "s1:v", "s2b:g", "s3:d0", "s2a:g", "s2b:v", "s4:l1", "s3:q", "s1:k", "s2a:v", "s4:l2", "s3:g", "s4:d1",
    "s4:r2", "s2b:k", "s3:v", "s4:o", "s4:q", "s2a:k", "s3:k", "s4:g", "s4:v", "s4:d0", "s4:k", "s5:d1", "s5:d0",
)
NAMES = ("q", "k", "v", "g", "o", "l", "r", "d")


def mm(a, b):
    return jnp.dot(a, b, preferred_element_type=F32)


def mm_nt(a, b):
    return lax.dot_general(a, b, NT, preferred_element_type=F32)


def mm_tn(a, b):
    return lax.dot_general(a, b, TN, preferred_element_type=F32)


def halves(rows):
    first = (rows // 2 + 7) // 8 * 8
    return pl.ds(0, first), pl.ds(first, rows - first)


def loop(count, body):
    def step(index, carry):
        body(index)
        return carry

    lax.fori_loop(0, count, step, 0)


def slope(pre):
    sigma = jax.nn.sigmoid(pre)
    return sigma * (1.0 + pre * (1.0 - sigma))


def unit(values):
    return lax.rsqrt(jnp.mean(values * values, axis=-1, keepdims=True) + EPS)


def unit_back(values, grad):
    scale = unit(values)
    rows = values * scale
    return scale * (grad - rows * jnp.mean(grad * rows, axis=-1, keepdims=True))


class Piece:
    def __init__(self, name, start, size, rows):
        self.name, self.start, self.size, self.rows = name, start, size, rows
        self.down = name == "d"
        self.parts = halves(rows)

    def moved(self, ref, zz, yy, xx, core, part=None):
        cols = pl.ds(self.start, self.size)
        if not self.down:
            return ref.at[zz, yy, xx, core, slice(None) if part is None else self.parts[part], cols]
        first, size = (0, self.rows) if part is None else (self.parts[part].start, self.parts[part].size)
        return ref.at[zz, yy, xx, pl.ds(pl.multiple_of(core * self.rows + first, 8), size), cols]

    def summed(self, ref, zz, yy, xx, core, part=None):
        if not self.down:
            return self.moved(ref, zz, yy, xx, core, part)
        size = self.size // C
        first = 0
        if part is not None:
            size, first = size // 2, part * (size // 2)
        start = pl.multiple_of(self.start + core * (self.size // C) + first, 128)
        return ref.at[zz, yy, xx, :, pl.ds(start, size)]

    def shape(self, part=None):
        if self.down:
            return (C * self.rows, self.size // C // (1 if part is None else 2))
        return (self.rows if part is None else self.parts[part].size, self.size)


def plan(width, hidden, rows, rows_down):
    tiles = hidden // TILE
    firsts = [tiles * n // sum(PARTS) * TILE for n in (sum(PARTS[:i]) for i in range(len(PARTS) + 1))]
    parts = [(start, stop - start) for start, stop in zip(firsts, firsts[1:])]
    half = width // 2
    cuts = {n: (n, 0, width) for n in "kvqgo"} | {"d0": ("d", 0, half), "d1": ("d", half, half)}
    for i, part in enumerate(parts):
        cuts |= {"l%d" % i: ("l", *part), "r%d" % i: ("r", *part)}
    return {n: Piece(*part, rows_down if part[0] == "d" else rows) for n, part in cuts.items()}, parts


def layer_kernel(*refs, heads):
    refs = list(refs)
    take = lambda n: [refs.pop(0) for _ in range(n)]
    hid, cot, counts, starts, rates = take(5)
    chunk = dict(zip(NAMES, take(8)))
    out, grad_in = take(2)
    grad = dict(zip(NAMES, take(8)))
    tokens, width = hid.shape
    hidden = chunk["l"].shape[1]
    hd = width // heads
    pieces, parts = plan(width, hidden, chunk["q"].shape[0], chunk["d"].shape[0])
    count = len(pieces)
    held_by_name = lambda: dict(zip(pieces, take(count)))
    from_core, from_a, from_b = held_by_name(), held_by_name(), held_by_name()
    W = dict(zip(NAMES, take(8)))
    third_a, third_b, last = held_by_name(), held_by_name(), held_by_name()
    stage_s, stage_d, swap_out, swap_in = take(4)
    nin, q_act, k_act, v_act = take(4)
    pre = dict(zip("qkvg", take(4)))
    mixed, gated, stream, nmid, low = take(5)
    prod, gl, gr = take(3)
    acc, gmid = take(2)
    scores, graw = take(2)
    state, prior, later = take(3)
    fwd_out, fwd_in, bwd_out, bwd_in = take(4)
    own_sem, stage_sem, gs_sem, gr_sem, rs_sem, rr_sem, st_send, st_recv = take(8)
    assert not refs

    seq, fs = lax.axis_index("seq"), lax.axis_index("fsdp")
    z, y, x, c = seq // Y, seq % Y, fs // C, fs % C

    def dev(zz, yy, xx, cc):
        return (zz * Y + yy, xx * C + cc)

    x_peer, y_peer, core_peer = dev(z, y, 1 - x, c), dev(z, 1 - y, x, c), dev(z, y, x, 1 - c)
    barrier = pltpu.get_barrier_semaphore()
    z_peers = [dev((z + n) % Z, y, x, c) for n in range(1, Z)]
    greet = [x_peer, y_peer, core_peer, *z_peers]
    for peer in greet:
        pl.semaphore_signal(barrier, inc=1, device_id=peer, device_id_type=MESH)
    pl.semaphore_wait(barrier, len(greet))

    def remote(src, dst, send, recv, peer):
        return pltpu.make_async_remote_copy(
            src_ref=src, dst_ref=dst, send_sem=send, recv_sem=recv, device_id=peer, device_id_type=MESH
        )

    def arrived(ref, sem):
        pltpu.make_async_copy(ref, ref, sem).wait()

    every = slice(None)
    row = {n: i for i, n in enumerate(pieces)}
    sent = {n: [] for n in pieces}

    def put(n, lane, src, dst, peer):
        copy = remote(src, dst, gs_sem.at[row[n], lane], gr_sem.at[row[n], lane], peer)
        copy.start()
        sent[n].append(copy)

    def pass_on(n, lane, peer, *where):
        here = pieces[n].moved(W[pieces[n].name], *where)
        put(n, lane, here, here, peer)

    def await_(n, lane, *where):
        arrived(pieces[n].moved(W[pieces[n].name], *where), gr_sem.at[row[n], lane])

    def own_copy(n):
        p = pieces[n]
        mine = p.moved(W[p.name], z, y, x, c)
        return pltpu.make_async_copy(chunk[p.name].at[:, pl.ds(p.start, p.size)], mine, own_sem.at[row[n]])

    def g0(n):
        p = pieces[n]
        own_copy(n).start()
        src = chunk[p.name].at[:, pl.ds(p.start, p.size)]
        for peer in z_peers:
            put(n, 0, src, p.moved(W[p.name], z, y, x, c), peer)

    def g1(n):
        own_copy(n).wait()
        await_(n, 0, pl.ds(0, Z - 1), y, x, c)
        pass_on(n, 1, x_peer, every, y, x, c, 0)
        pass_on(n, 2, y_peer, every, y, x, c, 1)
        pass_on(n, 5, core_peer, every, y, x, c)

    def g2a(n):
        await_(n, 1, every, y, 1 - x, c, 0)
        pass_on(n, 3, y_peer, every, y, every, c, 0)
        pass_on(n, 5, core_peer, every, y, 1 - x, c, 0)

    def g2b(n):
        await_(n, 2, every, 1 - y, x, c, 1)
        pass_on(n, 4, x_peer, every, every, x, c, 1)
        pass_on(n, 5, core_peer, every, 1 - y, x, c, 1)

    def g3a(n):
        await_(n, 3, every, 1 - y, every, c, 0)
        pass_on(n, 5, core_peer, every, 1 - y, every, c, 0)

    def g3b(n):
        await_(n, 4, every, every, 1 - x, c, 1)
        pass_on(n, 5, core_peer, every, every, 1 - x, c, 1)

    def g4(n):
        await_(n, 5, every, every, every, 1 - c)

    def released(n):
        for copy in sent[n]:
            copy.wait_send()
        sent[n] = []

    pending = []

    def push(n, lane, src, dst, peer):
        copy = remote(src, dst, rs_sem.at[row[n], lane], rr_sem.at[row[n], lane], peer)
        copy.start()
        pending.append(copy)

    def s0(n):
        p = pieces[n]
        push(n, 0, p.summed(W[p.name], every, every, every, 1 - c), from_core[n], core_peer)

    def staged(p, *where, part=None):
        held = stage_d if p.down else stage_s
        rows, cols = p.shape(part)
        return held.at[(*where, pl.ds(0, rows), pl.ds(0, cols))]

    def plus(mine, other):
        mine[...] = mine[...] + other[...]

    def s1(n):
        p = pieces[n]
        arrived(from_core[n], rr_sem.at[row[n], 0])

        def load(zz):
            return pltpu.make_async_copy(from_core[n].at[zz], staged(p, zz, every, every), stage_sem.at[zz])

        for zz in range(Z):
            load(zz).start()
        for zz in range(Z):
            load(zz).wait()

            def add(i, zz=zz):
                yy, xx = i // X, i % X
                plus(p.summed(W[p.name], zz, yy, xx, c), staged(p, zz, yy, xx))

            loop(Y * X, add)
        push(n, 1, p.summed(W[p.name], every, 1 - y, every, c, 0), from_a[n], y_peer)
        push(n, 2, p.summed(W[p.name], every, every, 1 - x, c, 1), from_b[n], x_peer)

    def s2(n, part):
        p = pieces[n]
        held = (from_a, from_b)[part][n]
        arrived(held, rr_sem.at[row[n], 1 + part])

        def load(zz):
            return pltpu.make_async_copy(held.at[zz], staged(p, zz, part, every, part=part), stage_sem.at[zz])

        for zz in range(Z):
            load(zz).start()
        for zz in range(Z):
            load(zz).wait()

            def add(i, zz=zz):
                where = (zz, i, x) if part else (zz, y, i)
                plus(p.summed(W[p.name], *where, c, part), staged(p, zz, part, i, part=part))

            loop(X, add)

    def s2a(n):
        p = pieces[n]
        s2(n, 0)
        push(n, 3, p.summed(W[p.name], every, y, 1 - x, c, 0), third_a[n], x_peer)

    def s2b(n):
        p = pieces[n]
        s2(n, 1)
        push(n, 4, p.summed(W[p.name], every, 1 - y, x, c, 1), third_b[n], y_peer)

    def s3(n):
        p = pieces[n]
        arrived(third_a[n], rr_sem.at[row[n], 3])
        arrived(third_b[n], rr_sem.at[row[n], 4])

        def add(zz):
            plus(p.summed(W[p.name], zz, y, x, c, 0), third_a[n].at[zz])
            plus(p.summed(W[p.name], zz, y, x, c, 1), third_b[n].at[zz])

        loop(Z, add)
        for k, peer in enumerate(z_peers):
            push(n, 5, p.summed(W[p.name], (z + k + 1) % Z, y, x, c), last[n].at[k], peer)

    def s4(n):
        p = pieces[n]
        arrived(last[n], rr_sem.at[row[n], 5])
        total = p.summed(W[p.name], z, y, x, c)[...].astype(F32)
        for k in range(Z - 1):
            total = total + last[n][k].astype(F32)
        if not p.down:
            grad[p.name][:, pl.ds(p.start, p.size)] = total
            return
        place, size = p.start // p.size, p.size // C
        swap_out[place] = total.reshape(C, p.rows, size)
        push(n, 6, swap_out.at[place, 1 - c], swap_in.at[place], core_peer)
        here = pl.ds(pl.multiple_of(p.start + c * size, 128), size)
        grad["d"][:, here] = swap_out[place, c]

    def s5(n):
        p = pieces[n]
        place, size = p.start // p.size, p.size // C
        arrived(swap_in.at[place], rr_sem.at[row[n], 6])
        there = pl.ds(pl.multiple_of(p.start + (1 - c) * size, 128), size)
        grad["d"][:, there] = swap_in[place]

    W2 = {n: W[n].reshape(hidden if n == "d" else width, width if n in "qkvgod" else hidden) for n in NAMES}
    wide = width // TILE
    row_tile = 32
    row_tiles = tokens // row_tile
    length = counts[0, 0]
    keep = (1 - starts[0, 0]).astype(F32)

    def cols_of(j):
        return pl.ds(pl.multiple_of(j * TILE, TILE), TILE)

    def head_of(h):
        return pl.ds(pl.multiple_of(h * hd, hd), hd)

    def rows_of(i):
        return pl.ds(pl.multiple_of(i * row_tile, row_tile), row_tile)

    def token_mask(shape, offset=0):
        return lax.broadcasted_iota(jnp.int32, shape, 0) + offset < length

    def position(shape):
        return lax.broadcasted_iota(jnp.int32, shape, 0).astype(F32)

    def decay_in(rate):
        return jnp.exp(-(position((tokens, hd)) + 1.0) * rate)

    def decay_out(rate):
        return jnp.exp(-(tokens - 1.0 - position((tokens, hd))) * rate)

    def decay_mask(rate):
        shape = (tokens, tokens)
        gap = position(shape) - lax.broadcasted_iota(jnp.int32, shape, 1).astype(F32)
        return jnp.where(gap >= 0, jnp.exp(-jnp.maximum(gap, 0.0) * rate), 0.0)

    def prepare():
        def body(i):
            rows = rows_of(i)
            value = hid[rows, :].astype(F32)
            nin[rows, :] = (value * unit(value)).astype(BF)
            mask = token_mask((row_tile, width), i * row_tile)
            low[rows, :] = jnp.where(mask, cot[rows, :].astype(F32), 0.0).astype(BF)

        loop(row_tiles, body)

    def project(name):
        target = {"q": q_act, "k": k_act, "v": v_act}.get(name)

        def body(j):
            cols = cols_of(j)
            value = mm(nin[...], W2[name][:, cols])
            pre[name][:, cols] = value
            if target is not None:
                act = value * jax.nn.sigmoid(value)
                if name == "k":
                    act = jnp.where(token_mask((tokens, TILE)), act, 0.0)
                target[:, cols] = act.astype(BF)

        loop(wide, body)

    flag_rows = pl.ds(width, 8)

    def local_state():
        def body(h):
            cols = head_of(h)
            keys = k_act[:, cols].astype(F32) * decay_out(rates[h])
            value = mm_tn(keys.astype(BF), v_act[:, cols])
            state[head_of(h), :] = value
            fwd_out[0, head_of(h), :] = value.astype(BF)

        loop(heads, body)

    def local_mix():
        def body(h):
            cols = head_of(h)
            raw = mm_nt(q_act[:, cols], k_act[:, cols])
            value = (raw * decay_mask(rates[h])).astype(BF)
            scores[h] = value
            mixed[:, cols] = mm(value, v_act[:, cols])

        loop(heads, body)

    def boxes(way):
        return (fwd_out, fwd_in) if way > 0 else (bwd_out, bwd_in)

    def note(way, slot, into, peer):
        sends, receives = boxes(way)
        lane = into + (0 if way > 0 else 4)
        return remote(sends.at[slot], receives.at[into], st_send.at[lane], st_recv.at[lane], peer)

    def along(way, step):
        return dev((z + way * step) % Z, y, x, c)

    def place_of(way):
        return z if way > 0 else Z - 1 - z

    def second_of(way):
        return (y if way > 0 else 1 - y).astype(F32)

    def faded(h, blocks):
        return jnp.exp(jnp.full((1, hd), -1.0 * tokens * blocks, F32) * rates[h])

    def flag(ref, slot):
        return ref[slot, flag_rows, :].astype(F32)[0:1, :]

    def pair(way):
        sends, _ = boxes(way)
        sends[0, flag_rows, :] = jnp.full((8, hd), keep, F32).astype(BF)
        note(way, 0, 0, y_peer).start()

    def round_b(way):
        sends, receives = boxes(way)
        note(way, 0, 0, y_peer).wait_recv()
        second, theirs = second_of(way), flag(receives, 0)

        def body(h):
            rows, fade = head_of(h), faded(h, 1)
            own = second + (1.0 - second) * fade * theirs
            other = second * fade * keep + (1.0 - second)
            value = own * state[rows, :] + other * receives[0, rows, :].astype(F32)
            sends[1, rows, :] = value.astype(BF)

        loop(heads, body)
        sends[1, flag_rows, :] = sends[0, flag_rows, :] * receives[0, flag_rows, :]

        @pl.when(place_of(way) < Z - 1)
        def _():
            note(way, 1, 1, along(way, 1)).start()

        @pl.when(place_of(way) == 0)
        def _():
            note(way, 1, 3, along(way, 3)).start()

    def round_c(way):
        sends, receives = boxes(way)
        place = place_of(way)

        @pl.when(place > 0)
        def _():
            note(way, 1, 1, along(way, 1)).wait_recv()

        @pl.when(jnp.logical_and(place > 0, place < Z - 1))
        def _():
            mine = flag(sends, 1)

            def body(h):
                rows = head_of(h)
                before = receives[1, rows, :].astype(F32)
                sends[2, rows, :] = (sends[1, rows, :].astype(F32) + faded(h, 2) * mine * before).astype(BF)

            loop(heads, body)
            sends[2, flag_rows, :] = sends[1, flag_rows, :] * receives[1, flag_rows, :]
            note(way, 2, 2, along(way, 1)).start()

    def finish(way, target):
        _, receives = boxes(way)
        place, second, theirs = place_of(way), second_of(way), flag(receives, 0)
        own = keep if way > 0 else 1.0

        def fill(entering):
            def body(h):
                rows = head_of(h)
                value = second * receives[0, rows, :].astype(F32)
                if entering is not None:
                    value = value + (second * faded(h, 1) * theirs + (1.0 - second)) * entering(h, rows)
                target[rows, :] = (own * value).astype(BF)

            loop(heads, body)

        @pl.when(place == 0)
        def _():
            fill(None)

        @pl.when(place == 1)
        def _():
            fill(lambda h, rows: receives[1, rows, :].astype(F32))

        @pl.when(place >= 2)
        def _():
            note(way, 2, 2, along(way, 1)).wait_recv()

        @pl.when(place == 2)
        def _():
            fill(lambda h, rows: receives[2, rows, :].astype(F32))

        @pl.when(place == 3)
        def _():
            note(way, 1, 3, along(way, 3)).wait_recv()
            both = flag(receives, 2)
            fill(lambda h, rows: receives[2, rows, :].astype(F32) + faded(h, 4) * both * receives[3, rows, :].astype(F32))

    def told(way):
        note(way, 0, 0, y_peer).wait_send()

        @pl.when(place_of(way) < Z - 1)
        def _():
            note(way, 1, 1, along(way, 1)).wait_send()

        @pl.when(place_of(way) == 0)
        def _():
            note(way, 1, 3, along(way, 3)).wait_send()

        @pl.when(jnp.logical_and(place_of(way) > 0, place_of(way) < Z - 1))
        def _():
            note(way, 2, 2, along(way, 1)).wait_send()

    def add_prior():
        def body(h):
            cols = head_of(h)
            value = (q_act[:, cols].astype(F32) * decay_in(rates[h])).astype(BF)
            mixed[:, cols] = mixed[:, cols] + mm(value, prior[head_of(h), :])

        loop(heads, body)

    def gate():
        def body(i):
            rows = rows_of(i)
            value = mixed[rows, :]
            opened = pre["g"][rows, :]
            opened = opened * jax.nn.sigmoid(opened)
            gated[rows, :] = (value * unit(value) * opened).astype(BF)

        loop(row_tiles, body)

    def to_stream():
        def body(j):
            cols = cols_of(j)
            stream[:, cols] = hid[:, cols].astype(F32) + mm(gated[...], W2["o"][:, cols])

        loop(wide, body)

        def norm(i):
            rows = rows_of(i)
            value = stream[rows, :]
            nmid[rows, :] = (value * unit(value)).astype(BF)

        loop(row_tiles, norm)

    def ffn(part):
        (start, size), add = parts[part], part > 0
        tiles = size // TILE

        def units(t):
            cols = pl.ds(pl.multiple_of(start + t * TILE, TILE), TILE)
            here = cols_of(t)
            left, right = mm(nmid[...], W2["l"][:, cols]), mm(nmid[...], W2["r"][:, cols])
            back = mm_nt(low[...], W2["d"][cols, :])
            prod[:, here] = (left * right).astype(BF)
            gl[:, here] = (back * right).astype(BF)
            gr[:, here] = (back * left).astype(BF)

        loop(tiles, units)
        span, held = pl.ds(start, size), pl.ds(0, size)

        def back(j):
            cols = cols_of(j)
            value = mm_nt(gl[:, held], W2["l"][cols, span]) + mm_nt(gr[:, held], W2["r"][cols, span])
            gmid[:, cols] = gmid[:, cols] + value if add else value

        loop(wide, back)

    def ffn_out(part):
        (start, size), add = parts[part], part > 0
        span, held = pl.ds(start, size), pl.ds(0, size)

        def forth(j):
            cols = cols_of(j)
            value = mm(prod[:, held], W2["d"][span, cols])
            acc[:, cols] = acc[:, cols] + value if add else value

        loop(wide, forth)

    def term(name, rows_ref, cols_ref):
        released(name)
        p = pieces[name]

        def body(t):
            here = cols_of(t)
            cols = pl.ds(pl.multiple_of(p.start + t * TILE, TILE), TILE)
            W2[p.name][:, cols] = mm_tn(rows_ref[...], cols_ref[:, here]).astype(BF)

        loop(p.size // TILE, body)

    def term_down(part):
        released("d0")
        released("d1")
        start, size = parts[part]

        def body(t):
            rows = pl.ds(pl.multiple_of(start + t * TILE, TILE), TILE)
            W2["d"][rows, :] = mm_tn(prod[:, cols_of(t)], low[...]).astype(BF)

        loop(size // TILE, body)

    def finish_out():
        def body(i):
            rows = rows_of(i)
            value = stream[rows, :] + acc[rows, :]
            mask = token_mask((row_tile, width), i * row_tile)
            out[rows, :] = jnp.where(mask, value, 0.0).astype(BF)

        loop(row_tiles, body)

    def to_grad_stream():
        def body(i):
            rows = rows_of(i)
            value = low[rows, :].astype(F32) + unit_back(stream[rows, :], gmid[rows, :])
            gmid[rows, :] = value
            low[rows, :] = value.astype(BF)

        loop(row_tiles, body)

    def back_gated():
        def body(j):
            cols = cols_of(j)
            acc[:, cols] = mm_nt(low[...], W2["o"][cols, :])

        loop(wide, body)

    def back_gate():
        def body(i):
            rows = rows_of(i)
            value, opened, back = mixed[rows, :], pre["g"][rows, :], acc[rows, :]
            normed = value * unit(value)
            gated[rows, :] = (back * normed * slope(opened)).astype(BF)
            back = back * (opened * jax.nn.sigmoid(opened))
            nmid[rows, :] = unit_back(value, back).astype(BF)

        loop(row_tiles, body)

    def back_scores():
        def body(h):
            cols = head_of(h)
            grads = nmid[:, cols]
            value = mm_nt(grads, v_act[:, cols]) * decay_mask(rates[h])
            graw[h] = value.astype(BF)
            queries = (q_act[:, cols].astype(F32) * decay_in(rates[h])).astype(BF)
            value = mm_tn(queries, grads) * keep
            state[head_of(h), :] = value
            bwd_out[0, head_of(h), :] = value.astype(BF)

        loop(heads, body)

    def back_query():
        def body(h):
            cols = head_of(h)
            value = mm(graw[h], k_act[:, cols])
            value = value + decay_in(rates[h]) * mm_nt(nmid[:, cols], prior[head_of(h), :])
            prod[:, cols] = (value * slope(pre["q"][:, cols])).astype(BF)

        loop(heads, body)

    def back_key_value():
        def body(h):
            cols = head_of(h)
            fade = decay_out(rates[h])
            grads_later = later[head_of(h), :]
            value = mm_tn(graw[h], q_act[:, cols]) + fade * mm_nt(v_act[:, cols], grads_later)
            value = jnp.where(token_mask((tokens, hd)), value, 0.0)
            gl[:, cols] = (value * slope(pre["k"][:, cols])).astype(BF)
            value = mm_tn(scores[h], nmid[:, cols]) + fade * mm(k_act[:, cols], grads_later)
            gr[:, cols] = (value * slope(pre["v"][:, cols])).astype(BF)

        loop(heads, body)

    def back_normed(name, source, add):
        def body(j):
            cols = cols_of(j)
            value = mm_nt(source[:, pl.ds(0, width)], W2[name][cols, :])
            acc[:, cols] = acc[:, cols] + value if add else value

        loop(wide, body)

    def finish_grad():
        def body(i):
            rows = rows_of(i)
            grad_in[rows, :] = gmid[rows, :] + unit_back(hid[rows, :].astype(F32), acc[rows, :])

        loop(row_tiles, body)

    steps = {
        "prepare": prepare,
        "local_state": local_state,
        "local_mix": local_mix,
        "add_prior": add_prior,
        "gate": gate,
        "to_stream": to_stream,
        "finish_out": finish_out,
        "to_grad_stream": to_grad_stream,
        "back_gated": back_gated,
        "back_gate": back_gate,
        "back_scores": back_scores,
        "back_query": back_query,
        "back_kv": back_key_value,
        "finish_grad": finish_grad,
        "fin:1": lambda: finish(1, prior),
        "fin:-1": lambda: finish(-1, later),
        "bn:g": lambda: back_normed("g", gated, False),
        "bn:q": lambda: back_normed("q", prod, True),
        "bn:k": lambda: back_normed("k", gl, True),
        "bn:v": lambda: back_normed("v", gr, True),
        "term:o": lambda: term("o", gated, low),
        "term:g": lambda: term("g", nin, gated),
        "term:q": lambda: term("q", nin, prod),
        "term:k": lambda: term("k", nin, gl),
        "term:v": lambda: term("v", nin, gr),
    }
    named = {
        "g0": g0, "g1": g1, "g2a": g2a, "g2b": g2b, "g3a": g3a, "g3b": g3b, "g4": g4,
        "s0": s0, "s1": s1, "s2a": s2a, "s2b": s2b, "s3": s3, "s4": s4, "s5": s5,
        "project": project,
    }
    for way in (1, -1):
        steps["pair:%d" % way] = functools.partial(pair, way)
        steps["B:%d" % way] = functools.partial(round_b, way)
        steps["C:%d" % way] = functools.partial(round_c, way)
    for part in range(len(parts)):
        steps["ffn:%d" % part] = functools.partial(ffn, part)
        steps["ffn_out:%d" % part] = functools.partial(ffn_out, part)
        steps["term:l%d" % part] = functools.partial(term, "l%d" % part, nmid, gl)
        steps["term:r%d" % part] = functools.partial(term, "r%d" % part, nmid, gr)
        steps["term_d:%d" % part] = functools.partial(term_down, part)
    for step in ORDER:
        if step in steps:
            steps[step]()
        else:
            kind, piece = step.split(":")
            named[kind](piece)
    for n in pieces:
        released(n)
    for copy in pending:
        copy.wait_send()
    for way in (1, -1):
        told(way)


def fused(hid, counts, starts, rates, weights, cot):
    tokens, width = hid.shape
    heads, hidden = rates.shape[0], weights[5].shape[1]
    hd = width // heads
    pieces, parts = plan(width, hidden, weights[0].shape[0], weights[7].shape[0])
    widest = max(size for _, size in parts)
    pieces = list(pieces.items())
    shape = jax.ShapeDtypeStruct
    dma = pltpu.SemaphoreType.DMA
    out_shape = [shape((tokens, width), BF), shape((tokens, width), F32)]
    out_shape += [shape(w.shape, F32) for w in weights]
    visible = len(out_shape)
    out_shape += [shape((Z, Y, X) + p.shape(), BF) for _, p in pieces]
    out_shape += [shape((Z, X) + p.shape(0), BF) for _, p in pieces]
    out_shape += [shape((Z, Y) + p.shape(1), BF) for _, p in pieces]
    vmem = pltpu.VMEM
    tall, flat = weights[7].shape[0], weights[0].shape[0]
    scratch = [vmem((Z, Y, X, C) + w.shape, BF) for w in weights[:7]] + [vmem((Z, Y, X, C * tall, width), BF)]
    scratch += [vmem((Z,) + p.shape(0), BF) for _, p in pieces]
    scratch += [vmem((Z,) + p.shape(1), BF) for _, p in pieces]
    scratch += [vmem((Z - 1,) + p.shape(), BF) for _, p in pieces]
    scratch += [vmem((Z, Y, X, flat, max(widest, width)), BF), vmem((Z, Y, X, C * tall, width // 4), BF)]
    scratch += [vmem((2, C, tall, width // 4), F32), vmem((2, tall, width // 4), F32)]
    scratch += [vmem((tokens, width), BF)] * 4
    scratch += [vmem((tokens, width), F32)] * 4
    scratch += [vmem((tokens, width), kind) for kind in (F32, BF, F32, BF, BF)]
    scratch += [vmem((tokens, max(widest, width)), BF)] * 3
    scratch += [vmem((tokens, width), F32)] * 2
    scratch += [vmem((heads, tokens, tokens), BF)] * 2
    scratch += [vmem((width, hd), F32), vmem((width, hd), BF), vmem((width, hd), BF)]
    scratch += [vmem((n, width + 8, hd), BF) for n in (3, 4, 3, 4)]
    count = len(pieces)
    scratch += [dma((count,)), dma((2 * Z,)), dma((count, 6)), dma((count, 6)), dma((count, 7)), dma((count, 7))]
    scratch += [dma((8,)), dma((8,))]
    near, far = pl.BlockSpec(memory_space=pltpu.VMEM), pl.BlockSpec(memory_space=pl.ANY)
    small = pl.BlockSpec(memory_space=pltpu.SMEM)
    flops = 6 * tokens * sum(w.shape[0] * w.shape[1] * Z * Y * X * C for w in weights)
    results = pl.pallas_call(
        functools.partial(layer_kernel, heads=heads),
        out_shape=out_shape,
        in_specs=[near, near, small, small, small] + [far] * 8,
        out_specs=[near] * visible + [far] * (len(out_shape) - visible),
        scratch_shapes=scratch,
        compiler_params=pltpu.CompilerParams(
            collective_id=0, has_side_effects=True, vmem_limit_bytes=67043328
        ),
        cost_estimate=pl.CostEstimate(flops=flops, bytes_accessed=60000000, transcendentals=0),
    )(hid, cot, counts, starts, rates, *weights)
    return results[:visible]


def entering(value, axis, join, neutral):
    count, mine = (lax.axis_size(axis), lax.axis_index(axis))
    pieces = jax.tree.map(lambda part: lax.all_gather(part, axis), value)
    running = jax.tree.map(
        lambda part, zero: jnp.full_like(part, 0) + jnp.asarray(zero, part.dtype), value, neutral
    )

    def hop(position, running):
        longer = join(running, jax.tree.map(lambda part: part[position], pieces))
        return jax.tree.map(lambda new, old: jnp.where(position < mine, new, old), longer, running)

    return lax.fori_loop(0, count - 1, hop, running)


def carried_in(x, axis, join, neutral):
    count = lax.axis_size(axis)
    place = lax.axis_index(axis)
    ahead = count - 1 - place
    gathered = jax.tree.map(
        lambda a, kind: lax.all_gather(a.astype(kind), axis), x, (jnp.bfloat16, jnp.bfloat16)
    )
    state = jax.tree.map(lambda a, e: jnp.zeros_like(a) + jnp.asarray(e, a.dtype), x, neutral)

    def one(hop, state):
        source = count - 1 - hop
        return join(
            state,
            jax.tree.map(
                lambda a, own: lax.dynamic_index_in_dim(a, source, 0, False).astype(own.dtype),
                gathered,
                x,
            ),
        )

    return lax.fori_loop(0, ahead, one, state)


def rms_norm(values):
    return values * lax.rsqrt(jnp.mean(values * values, axis=-1, keepdims=True) + EPS)


def norm_back(values, grad_norm):
    _, pull = jax.vjp(rms_norm, values)
    return pull(grad_norm)[0]


def silu_slope(values):
    sigma = jax.nn.sigmoid(values)
    return sigma * (1.0 + values * (1.0 - sigma))


def affine_join(earlier, later):
    return (earlier[0] * later[0], later[0][:, None, None] * earlier[1] + later[1])


def matmul(left, right):
    return jnp.dot(left, right, preferred_element_type=jnp.float32)


def matmul_left_t(left, right):
    return jnp.einsum("ab,ac->bc", left, right, preferred_element_type=jnp.float32)


def matmul_right_t(left, right):
    return jnp.einsum("ab,cb->ac", left, right, preferred_element_type=jnp.float32)


def precise(form, left, right):
    return jnp.einsum(form, left, right, precision=lax.Precision.HIGHEST)


def fits(hidden_in, decay_rates, weights):
    mesh = (lax.axis_size("seq"), lax.axis_size("fsdp"))
    tiles = weights[0].shape[0] % 16 == 0 and weights[7].shape[0] % 8 == 0
    head = hidden_in.shape[2] // decay_rates.shape[0]
    return mesh == (SEQ, FSDP) and tiles and hidden_in.shape[1] == TILE and head % 128 == 0


def on_device(
    hidden_in,
    block_counts,
    seq_starts,
    decay_rates,
    w_query,
    w_key,
    w_value,
    w_gate,
    w_out,
    w_left,
    w_right,
    w_down,
    cotangent,
):
    weights = (w_query, w_key, w_value, w_gate, w_out, w_left, w_right, w_down)
    if fits(hidden_in, decay_rates, weights):
        results = fused(hidden_in[0], block_counts, seq_starts, decay_rates, weights, cotangent[0])
        return (results[0][None], results[1][None], *results[2:])
    tok_rows = hidden_in.shape[1]
    width = hidden_in.shape[2]
    heads = decay_rates.shape[0]
    head_dim = width // heads
    blocks = block_counts.shape[1]
    block_len = tok_rows // blocks
    residual_in = hidden_in[0].astype(jnp.float32)
    offsets = jnp.arange(block_len)
    token_mask = (offsets[None, :] < block_counts[0][:, None]).astype(jnp.float32).reshape(tok_rows)
    keep_state = (1 - seq_starts[0]).astype(jnp.float32)
    position = offsets.astype(jnp.float32)
    decay_in = jnp.exp(-(position[:, None] + 1.0) * decay_rates[None, :])
    decay_out = jnp.exp(-(block_len - 1.0 - position[:, None]) * decay_rates[None, :])
    decay_block = jnp.exp(-block_len * decay_rates)
    distance = position[:, None] - position[None, :]
    decay_mask = jnp.where(
        distance[None] >= 0,
        jnp.exp(-jnp.maximum(distance, 0.0)[None] * decay_rates[:, None, None]),
        0.0,
    )
    shape_four = (blocks, block_len, heads, head_dim)
    identity = (
        jnp.ones((heads,), jnp.float32),
        jnp.zeros((heads, head_dim, head_dim), jnp.float32),
    )
    attn_full = (
        lax.all_gather(w_query, ("seq", "fsdp"), axis=0, tiled=True),
        lax.all_gather(w_key, ("seq", "fsdp"), axis=0, tiled=True),
        lax.all_gather(w_value, ("seq", "fsdp"), axis=0, tiled=True),
        lax.all_gather(w_gate, ("seq", "fsdp"), axis=0, tiled=True),
        lax.all_gather(w_out, ("seq", "fsdp"), axis=0, tiled=True),
    )
    normed_in = rms_norm(residual_in).astype(jnp.bfloat16)
    query_pre = matmul(normed_in, attn_full[0])
    key_pre = matmul(normed_in, attn_full[1])
    value_pre = matmul(normed_in, attn_full[2])
    gate_pre = matmul(normed_in, attn_full[3])
    query_rows = jax.nn.silu(query_pre).astype(jnp.bfloat16)
    key_rows = (jax.nn.silu(key_pre) * token_mask[:, None]).astype(jnp.bfloat16)
    value_rows = jax.nn.silu(value_pre).astype(jnp.bfloat16)
    gate_rows = jax.nn.silu(gate_pre)
    query_blk = query_rows.reshape(shape_four)
    key_blk = key_rows.reshape(shape_four)
    value_blk = value_rows.reshape(shape_four)
    key_full = key_blk.astype(jnp.float32)
    value_full = value_blk.astype(jnp.float32)
    query_decay = query_blk.astype(jnp.float32) * decay_in[None, :, :, None]
    key_decay = key_full * decay_out[None, :, :, None]
    local_states = precise("bthd,bthe->bhde", key_decay, value_full)
    carry_scale = identity[0]
    carry_state = identity[1]
    number = 0
    factor = keep_state[number] * decay_block
    carry_scale = carry_scale * factor
    carry_state = factor[:, None, None] * carry_state + local_states[number]
    arrived = entering((carry_scale, carry_state), "seq", affine_join, identity)
    state_now = arrived[1]
    number = 0
    prior = keep_state[number] * state_now
    priors = [prior]
    prior_states = jnp.stack(priors)
    raw_scores = jnp.einsum(
        "bthd,bshd->bhts", query_blk, key_blk, preferred_element_type=jnp.float32
    )
    scores = (raw_scores * decay_mask[None]).astype(jnp.bfloat16)
    intra = jnp.einsum("bhts,bshd->bthd", scores, value_blk, preferred_element_type=jnp.float32)
    inter = precise("bthd,bhde->bthe", query_decay, prior_states)
    mixed = (intra + inter).reshape(tok_rows, width)
    mixed_norm = rms_norm(mixed)
    gated = (mixed_norm * gate_rows).astype(jnp.bfloat16)
    stream = residual_in + matmul(gated, attn_full[4])
    ffn_full = (
        lax.all_gather(w_left, ("seq", "fsdp"), axis=0, tiled=True),
        lax.all_gather(w_right, ("seq", "fsdp"), axis=0, tiled=True),
        lax.all_gather(w_down, ("seq", "fsdp"), axis=0, tiled=True),
    )
    normed_mid = rms_norm(stream).astype(jnp.bfloat16)
    left_pre = matmul(normed_mid, ffn_full[0])
    right_pre = matmul(normed_mid, ffn_full[1])
    product = (left_pre * right_pre).astype(jnp.bfloat16)
    output = (token_mask[:, None] * (stream + matmul(product, ffn_full[2]))).astype(jnp.bfloat16)
    grad_rows = cotangent[0].astype(jnp.float32) * token_mask[:, None]
    grad_low = grad_rows.astype(jnp.bfloat16)
    ffn_back = (
        lax.all_gather(w_left, ("seq", "fsdp"), axis=0, tiled=True),
        lax.all_gather(w_right, ("seq", "fsdp"), axis=0, tiled=True),
        lax.all_gather(w_down, ("seq", "fsdp"), axis=0, tiled=True),
    )
    grad_product = matmul_right_t(grad_low, ffn_back[2])
    grad_left = (grad_product * right_pre).astype(jnp.bfloat16)
    grad_right = (grad_product * left_pre).astype(jnp.bfloat16)
    term_down = matmul_left_t(product, grad_low)
    term_left = matmul_left_t(normed_mid, grad_left)
    term_right = matmul_left_t(normed_mid, grad_right)
    grad_mid = matmul_right_t(grad_left, ffn_back[0]) + matmul_right_t(grad_right, ffn_back[1])
    ffn_grads = (
        lax.psum_scatter(term_left, ("seq", "fsdp"), scatter_dimension=0, tiled=True),
        lax.psum_scatter(term_right, ("seq", "fsdp"), scatter_dimension=0, tiled=True),
        lax.psum_scatter(term_down, ("seq", "fsdp"), scatter_dimension=0, tiled=True),
    )
    grad_stream = grad_rows + norm_back(stream, grad_mid)
    grad_stream_low = grad_stream.astype(jnp.bfloat16)
    attn_back = (
        lax.all_gather(w_query, ("seq", "fsdp"), axis=0, tiled=True),
        lax.all_gather(w_key, ("seq", "fsdp"), axis=0, tiled=True),
        lax.all_gather(w_value, ("seq", "fsdp"), axis=0, tiled=True),
        lax.all_gather(w_gate, ("seq", "fsdp"), axis=0, tiled=True),
        lax.all_gather(w_out, ("seq", "fsdp"), axis=0, tiled=True),
    )
    term_out = matmul_left_t(gated, grad_stream_low)
    grad_gated = matmul_right_t(grad_stream_low, attn_back[4])
    grad_gate_rows = grad_gated * mixed_norm
    grad_mixed = norm_back(mixed, grad_gated * gate_rows)
    grad_mix_blk = grad_mixed.astype(jnp.bfloat16).reshape(shape_four)
    grad_mix_full = grad_mix_blk.astype(jnp.float32)
    grad_scores = jnp.einsum(
        "bthe,bshe->bhts", grad_mix_blk, value_blk, preferred_element_type=jnp.float32
    )
    grad_raw = (grad_scores * decay_mask[None]).astype(jnp.bfloat16)
    grad_prior = precise("bthd,bthe->bhde", query_decay, grad_mix_full)
    back_state = identity[1]
    for number in reversed(range(blocks)):
        back_state = keep_state[number] * (
            grad_prior[number] + decay_block[:, None, None] * back_state
        )
    arriving = carried_in((carry_scale, back_state), "seq", affine_join, identity)
    later_grad = arriving[1]
    state_list = [later_grad] * blocks
    for number in reversed(range(blocks)):
        state_list[number] = later_grad
        later_grad = keep_state[number] * (
            grad_prior[number] + decay_block[:, None, None] * later_grad
        )
    state_grads = jnp.stack(state_list)
    query_grad = jnp.einsum(
        "bhts,bshd->bthd", grad_raw, key_blk, preferred_element_type=jnp.float32
    )
    query_grad = query_grad + decay_in[None, :, :, None] * precise(
        "bthe,bhde->bthd", grad_mix_full, prior_states
    )
    key_grad = jnp.einsum(
        "bhts,bthd->bshd", grad_raw, query_blk, preferred_element_type=jnp.float32
    )
    key_grad = key_grad + decay_out[None, :, :, None] * precise(
        "bthe,bhde->bthd", value_full, state_grads
    )
    value_grad = jnp.einsum(
        "bhts,bthe->bshe", scores, grad_mix_blk, preferred_element_type=jnp.float32
    )
    value_grad = value_grad + decay_out[None, :, :, None] * precise(
        "bthd,bhde->bthe", key_full, state_grads
    )
    grad_query_pre = (query_grad.reshape(tok_rows, width) * silu_slope(query_pre)).astype(
        jnp.bfloat16
    )
    grad_key_pre = (
        key_grad.reshape(tok_rows, width) * token_mask[:, None] * silu_slope(key_pre)
    ).astype(jnp.bfloat16)
    grad_value_pre = (value_grad.reshape(tok_rows, width) * silu_slope(value_pre)).astype(
        jnp.bfloat16
    )
    grad_gate_pre = (grad_gate_rows * silu_slope(gate_pre)).astype(jnp.bfloat16)
    term_query = matmul_left_t(normed_in, grad_query_pre)
    term_key = matmul_left_t(normed_in, grad_key_pre)
    term_value = matmul_left_t(normed_in, grad_value_pre)
    term_gate = matmul_left_t(normed_in, grad_gate_pre)
    grad_normed = matmul_right_t(grad_query_pre, attn_back[0]) + matmul_right_t(
        grad_key_pre, attn_back[1]
    )
    grad_normed = (
        grad_normed
        + matmul_right_t(grad_value_pre, attn_back[2])
        + matmul_right_t(grad_gate_pre, attn_back[3])
    )
    attn_grads = (
        lax.psum_scatter(term_query, ("seq", "fsdp"), scatter_dimension=0, tiled=True),
        lax.psum_scatter(term_key, ("seq", "fsdp"), scatter_dimension=0, tiled=True),
        lax.psum_scatter(term_value, ("seq", "fsdp"), scatter_dimension=0, tiled=True),
        lax.psum_scatter(term_gate, ("seq", "fsdp"), scatter_dimension=0, tiled=True),
        lax.psum_scatter(term_out, ("seq", "fsdp"), scatter_dimension=0, tiled=True),
    )
    grad_input = grad_stream + norm_back(residual_in, grad_normed)
    return (
        output[None],
        grad_input[None],
        attn_grads[0],
        attn_grads[1],
        attn_grads[2],
        attn_grads[3],
        attn_grads[4],
        ffn_grads[0],
        ffn_grads[1],
        ffn_grads[2],
    )


def solution(mesh):
    return jax.shard_map(
        on_device,
        mesh=mesh,
        in_specs=(
            P("fsdp", "seq", None),
            P("fsdp", "seq"),
            P("fsdp", "seq"),
            P(),
            P(("seq", "fsdp"), None),
            P(("seq", "fsdp"), None),
            P(("seq", "fsdp"), None),
            P(("seq", "fsdp"), None),
            P(("seq", "fsdp"), None),
            P(("seq", "fsdp"), None),
            P(("seq", "fsdp"), None),
            P(("seq", "fsdp"), None),
            P("fsdp", "seq", None),
        ),
        out_specs=(
            P("fsdp", "seq", None),
            P("fsdp", "seq", None),
            P(("seq", "fsdp"), None),
            P(("seq", "fsdp"), None),
            P(("seq", "fsdp"), None),
            P(("seq", "fsdp"), None),
            P(("seq", "fsdp"), None),
            P(("seq", "fsdp"), None),
            P(("seq", "fsdp"), None),
            P(("seq", "fsdp"), None),
        ),
        check_vma=False,
    )
```
